32 devices in a mesh: slab: 2 (over y), date: 4 (over z), rng: 2 (over x), az: 2 (over core).
Axes of the slice: x: 2, y: 2, z: 4, core: 2. Of those that a mesh axis runs over, the one named last changes fastest.
Arguments:
- slc: bfloat16 [64, 2, 128, 512], P(('slab', 'date'), None, 'az', 'rng'), parts along dimension 0, may hold values from -30 to 30
- lags: int32 [32, 6], P('date'), may hold values from 0 to 8, as said below
Outputs:
- coherence: bfloat16 [64, 6, 128, 512], P(('slab', 'date'), None, 'az', 'rng'), parts along dimension 0
- log_ratio: bfloat16 [64, 6, 128, 512], P(('slab', 'date'), None, 'az', 'rng'), parts along dimension 0
- quegan: float32 [64, 128, 512], P(('slab', 'date'), 'az', 'rng'), parts along dimension 0
The draws below stay inside these ranges and needn't reach their ends.
There are 2 independent parts, one for each index of `slab`. The reference program is written for one: setup_inputs(seed, part) draws one part's arguments, and reference() takes and returns one part's arrays. A program takes and returns all parts, laid end to end along the dimension named above; an argument that names none is the same for every part. Nothing has to cross between parts.
Inputs may be any that keep to these rules, and one draw needn't show every extreme that they name: Each entry is 0 (no partner) or a lag with date + lag < 32; the nonzero lags of one date are distinct; date 0 lists 6 partners, one of them at lag 8.
All inputs are finite; a program needn't handle non-finite values.
Results may differ from the reference program's by a relative error of at most 0.012.
Values may be sent and summed in bfloat16 or wider, within the bound.
A program may use at most 64 MiB of HBM per device.

```python
import jax
import jax.numpy as jnp
from jax import lax

SLOTS = 6
HALF_AZ = 2
HALF_RG = 10
LAG_MAX = 8
DATES = 32
LINES = 128
COLS = 512


def draw_slc(key, part):
    keys = jax.random.split(jax.random.fold_in(key, 11), 4)
    common = jnp.clip(jax.random.normal(keys[0], (1, 2, LINES, COLS), jnp.float32), -5.0, 5.0) * 0.7071
    own = jnp.clip(jax.random.normal(keys[1], (DATES, 2, LINES, COLS), jnp.float32), -5.0, 5.0) * 0.7071
    rho = jax.random.uniform(keys[2], (DATES, 1, 1, 1), jnp.float32, 0.3, 0.9)
    texture = jnp.exp(0.4 * jnp.clip(jax.random.normal(keys[3], (DATES, 1, LINES, COLS), jnp.float32), -3.0, 3.0))
    fields = texture * (jnp.sqrt(rho) * common + jnp.sqrt(1.0 - rho) * own)
    return jnp.clip(fields, -30.0, 30.0).astype(jnp.bfloat16)


def draw_lags(key, part):
    keys = jax.random.split(jax.random.fold_in(key, 23), 2)
    scores = jax.random.randint(keys[0], (DATES, LAG_MAX), 0, 1 << 20) * LAG_MAX + jnp.arange(LAG_MAX, dtype=jnp.int32)[None, :]
    order = jnp.argsort(scores, axis=1, stable=True)
    picked = (order[:, :SLOTS] + 1).astype(jnp.int32)
    counts = jax.random.randint(keys[1], (DATES, 1), 2, SLOTS + 1)
    slot_ids = jnp.arange(SLOTS, dtype=jnp.int32)[None, :]
    date_ids = jnp.arange(DATES, dtype=jnp.int32)[:, None]
    picked = jnp.where(date_ids == 0, LAG_MAX - slot_ids, picked)
    counts = jnp.where(date_ids == 0, SLOTS, counts)
    live_slots = (slot_ids < counts) & (date_ids + picked < DATES)
    return jnp.where(live_slots, picked, 0).astype(jnp.int32)


def setup_inputs(seed: int = 0, part: int = 0) -> dict:
    seeds = jax.random.split(jax.random.key(seed), 3)
    part_splits = jax.random.split(jax.random.fold_in(seeds[2], part), 3)
    return {
        "slc": draw_slc(jax.random.fold_in(jax.random.fold_in(seeds[2], part), 71), part),
        "lags": draw_lags(jax.random.fold_in(seeds[2], 71), part),
    }


EPS = 1e-5


def box_mean(fields):
    line_count = fields.shape[-2]
    column_count = fields.shape[-1]
    pad_width = [(0, 0)] * (fields.ndim - 2) + [(HALF_AZ, HALF_AZ), (HALF_RG, HALF_RG)]
    padded = jnp.pad(fields, pad_width)
    row_sums = padded[..., 0:line_count, :]
    for offset in range(1, 2 * HALF_AZ + 1):
        row_sums = row_sums + padded[..., offset:offset + line_count, :]
    totals = row_sums[..., :, 0:column_count]
    for offset in range(1, 2 * HALF_RG + 1):
        totals = totals + row_sums[..., :, offset:offset + column_count]
    return totals / float((2 * HALF_AZ + 1) * (2 * HALF_RG + 1))


def reference(slc, lags):
    fields = slc.astype(jnp.float32)
    powers = fields[:, 0] ** 2 + fields[:, 1] ** 2
    mean_power = lax.map(box_mean, powers) + EPS
    ratio_sum = jnp.sum(powers / mean_power, axis=0)
    quegan = mean_power * ratio_sum / float(DATES)

    def one_date(packed):
        date_index, lag_row = packed
        live_slots = lag_row > 0
        partners = (date_index + jnp.where(live_slots, lag_row, 0)).astype(jnp.int32)
        own_tile = fields[date_index]
        second = fields[partners]
        cross_re = own_tile[0][None] * second[:, 0] + own_tile[1][None] * second[:, 1]
        cross_im = own_tile[1][None] * second[:, 0] - own_tile[0][None] * second[:, 1]
        boxed_cross = box_mean(jnp.stack([cross_re, cross_im]))
        own_mean = mean_power[date_index][None]
        partner_mean = mean_power[partners]
        coherence = (boxed_cross[0] ** 2 + boxed_cross[1] ** 2) / (own_mean * partner_mean)
        log_ratio = jnp.log(own_mean / partner_mean)
        slot_mask = live_slots[:, None, None]
        return (jnp.where(slot_mask, coherence, 0.0).astype(jnp.bfloat16),
                jnp.where(slot_mask, log_ratio, 0.0).astype(jnp.bfloat16))

    coherence, log_ratio = lax.map(one_date, (jnp.arange(DATES, dtype=jnp.int32), lags))
    return coherence, log_ratio, quegan
```

```python
import functools

import jax
import jax.numpy as jnp
from jax import lax
from jax.experimental import pallas as pl
from jax.experimental.pallas import tpu as pltpu
from jax.sharding import PartitionSpec as P

HALF_AZ = 2
HALF_RG = 10
LAG_MAX = 8
EPS = 1e-05
LOOKS = float((2 * HALF_AZ + 1) * (2 * HALF_RG + 1))

LANES = 128
ROWS = 16
EDGE = 16
PARTS = 2
BLOCKS = 2
LP = True
DEPTH = 1
GROUP = LANES // (EDGE * PARTS)
BATCH = 4
VMEM_BYTES = 67043328
SPARE = 16 * 2 ** 20
F32 = jnp.float32
BF16 = jnp.bfloat16

ORDER = [
    "X0 Sp0 Sf2 P0",
    "P1 P2 P3 P4",
    "P5 P6 P7 K0",
    "Sf3 Sb1 Sf4 Q1",
    "Q2 Q3 Q4 B0",
    "Q5 Q6 Q7 V0",
    "U0 F0 P8 Q8",
    "K1 Sf5 Sf6 Sf7",
    "F1 P9 Q9 F2",
    "P10 Q10 F3 P11",
    "Q11 B1 V1 F4",
    "P12 Q12 K2 F5",
    "P13 Q13 F6 P14",
    "Q14 F7 P15 Q15",
    "K3 T",
]
ORDER = [word for words in ORDER for word in words.split()]
FIRST = ["Sb0", "Sf0", "Sf1"]


def gather_kernel(sizes, slc, lags_in, coh, logs, queg, lags,
                  tiles, packs_out, packs_in, edges, edge_power, edge_cross, band, diag, pick, inv, mean, acc, chain_out, chain_in,
                  own_sem, lag_sem, z_send, z_recv, a_send, a_recv, x_send, x_recv,
                  c_send, c_recv):
    dates_axis, rng_axis, dates, lines, cols = sizes
    sides = 1 if rng_axis == 2 else 2
    groups = dates // GROUP
    date = lax.axis_index("date")
    rng = lax.axis_index("rng")
    az = lax.axis_index("az")
    has_next = date < dates_axis - 1
    has_prev = date > 0
    has_right = rng < rng_axis - 1
    has_left = rng > 0
    peer = 1 - az
    height = lines + ROWS

    barrier = pltpu.get_barrier_semaphore()

    def greet(where):
        pl.semaphore_signal(barrier, inc=1, device_id=where, device_id_type=pl.DeviceIdType.MESH)

    greet({"az": peer})
    pl.when(has_prev)(lambda: greet({"date": date - 1}))
    pl.when(has_next)(lambda: greet({"date": date + 1}))
    pl.when(has_left)(lambda: greet({"rng": rng - 1}))
    pl.when(has_right)(lambda: greet({"rng": rng + 1}))

    def block_of(b):
        return pl.ds(b * LANES if isinstance(b, int) else pl.multiple_of(b * LANES, LANES), LANES)

    own = [
        pltpu.make_async_copy(
            slc.at[:, :, :, block_of(b)], tiles.at[pl.ds(0, dates), :, b, pl.ds(0, lines), :], own_sem.at[b])
        for b in range(BLOCKS)]
    for copy in own:
        copy.start()
    lag_copy = pltpu.make_async_copy(lags_in, lags, lag_sem)
    lag_copy.start()

    border = pl.multiple_of((1 - az) * (lines - ROWS), ROWS)
    rest = pl.multiple_of(az * ROWS, ROWS)

    def z_copies(piece, to):
        kind, i = piece[0], int(piece[1:])
        if kind == "p":
            return [pltpu.make_async_remote_copy(
                src_ref=packs_in.at[0], dst_ref=packs_in.at[1],
                send_sem=z_send.at[0, 0], recv_sem=z_recv.at[0, 0],
                device_id={"date": to}, device_id_type=pl.DeviceIdType.MESH)]
        if kind == "b":
            first, count, row, rows, k = i * GROUP, GROUP, border, ROWS, 1 + i
        else:
            first, count, row, rows, k = i, 1, rest, lines - ROWS, 1 + groups + i
        return [
            pltpu.make_async_remote_copy(
                src_ref=slc.at[pl.ds(first, count), :, pl.ds(row, rows), block_of(b)],
                dst_ref=tiles.at[pl.ds(dates + first, count), :, b, pl.ds(row, rows), :],
                send_sem=z_send.at[k, b], recv_sem=z_recv.at[k, b],
                device_id={"date": to}, device_id_type=pl.DeviceIdType.MESH)
            for b in range(BLOCKS)]

    own_rows = [
        pltpu.make_async_remote_copy(
            src_ref=slc.at[:, :, pl.ds(border, ROWS), block_of(b)],
            dst_ref=tiles.at[pl.ds(0, dates), :, b, pl.ds(lines, ROWS), :],
            send_sem=a_send.at[0, b], recv_sem=a_recv.at[0, b],
            device_id={"az": peer}, device_id_type=pl.DeviceIdType.MESH)
        for b in range(BLOCKS)]

    def a_copies(g):
        where = pl.ds(dates + g * GROUP, GROUP)
        return [
            pltpu.make_async_remote_copy(
                src_ref=tiles.at[where, :, b, pl.ds(border, ROWS), :],
                dst_ref=tiles.at[where, :, b, pl.ds(lines, ROWS), :],
                send_sem=a_send.at[1 + g, b], recv_sem=a_recv.at[1 + g, b],
                device_id={"az": peer}, device_id_type=pl.DeviceIdType.MESH)
            for b in range(BLOCKS)]

    def x_copy(g, tail, side, to):
        rows = pl.ds(lines, ROWS) if tail else pl.ds(0, lines)
        return pltpu.make_async_remote_copy(
            src_ref=packs_out.at[g, side, rows, :],
            dst_ref=packs_in.at[0, g, side, rows, :],
            send_sem=x_send.at[side, g, tail], recv_sem=x_recv.at[side, g, tail],
            device_id={"rng": to}, device_id_type=pl.DeviceIdType.MESH)

    def x_each(g, tail, act):
        if sides == 1:
            act(x_copy(g, tail, 0, 1 - rng))
        else:
            pl.when(has_right)(lambda: act(x_copy(g, tail, 0, rng + 1)))
            pl.when(has_left)(lambda: act(x_copy(g, tail, 1, rng - 1)))

    def x_wait(g):
        for tail in range(2):
            if sides == 1:
                x_copy(g, tail, 0, 1 - rng).wait_recv()
            else:
                pl.when(has_left)(lambda: x_copy(g, tail, 0, rng - 1).wait_recv())
                pl.when(has_right)(lambda: x_copy(g, tail, 1, rng + 1).wait_recv())

    def left_of(side):
        return rng if sides == 1 else 1 - side

    def slot_of(lane, left):
        return lax.shift_right_logical((lane + EDGE * left) & (LANES - 1), EDGE.bit_length() - 1)

    def pack(g, tail):
        first, rows = (lines, ROWS) if tail else (0, lines)
        lane = lax.broadcasted_iota(jnp.int32, (rows, LANES), 1)
        for side in range(sides):
            high = 1 - rng if sides == 1 else 1 - side
            block = 1 - rng if sides == 1 else (1 - side) * (BLOCKS - 1)
            slot = slot_of(lane, high)
            out = None
            for s in range(GROUP * PARTS):
                x = tiles[g * GROUP + s % GROUP, s // GROUP, block, first:first + rows, :].astype(F32)
                out = x if s == 0 else jnp.where(slot == s, pltpu.roll(x, EDGE * s, axis=1), out)
            packs_out[g, side, first:first + rows] = out.astype(BF16)
        x_each(g, tail, lambda c: c.start())

    def unpack(late):
        lane = lax.broadcasted_iota(jnp.int32, (height, LANES), 1)
        for side in range(sides):
            lower = slot_of(lane, left_of(side)) < GROUP
            x = packs_in[late, 0, side].astype(F32)
            y = packs_in[late, 1, side].astype(F32)
            edges[late, side, 0] = jnp.where(lower, x, pltpu.roll(y, LANES // 2, axis=1)).astype(BF16)
            edges[late, side, 1] = jnp.where(lower, pltpu.roll(x, LANES // 2, axis=1), y).astype(BF16)

    if sides == 2:
        @pl.when(rng == 0)
        def _():
            packs_in[0, :, 0] = jnp.zeros((groups, height, LANES), BF16)

        @pl.when(rng == rng_axis - 1)
        def _():
            packs_in[0, :, 1] = jnp.zeros((groups, height, LANES), BF16)

    peers = 1
    for cond in (has_prev, has_next, has_left, has_right):
        peers = peers + cond.astype(jnp.int32)
    pl.semaphore_wait(barrier, peers)

    def send(pieces):
        @pl.when(has_prev)
        def _():
            for piece in pieces:
                for copy in z_copies(piece, date - 1):
                    copy.start()

    send([word[1:] for word in FIRST])
    for copy in own_rows:
        copy.start()
    for copy in own:
        copy.wait()
    for g in range(groups):
        pack(g, 0)

    @pl.when(date == dates_axis - 1)
    def _():
        tiles[dates:] = jnp.zeros((dates, PARTS, BLOCKS, height, LANES), BF16)
        packs_in[1] = jnp.zeros((groups, sides, height, LANES), BF16)

    frame = (1 - rng, rng) if sides == 1 else tuple(range(BLOCKS))

    def column_of(index):
        return jnp.where(index < LANES, LANES * frame[0], LANES * (frame[1] - 1)) + index

    col_out = column_of(lax.broadcasted_iota(jnp.int32, (cols, cols), 1))
    col_in = column_of(lax.broadcasted_iota(jnp.int32, (cols, cols), 0))
    band[...] = (jnp.abs(col_in - col_out) <= HALF_RG).astype(F32).astype(BF16)
    edge_in = lax.broadcasted_iota(jnp.int32, (LANES, LANES), 0)
    edge_out = lax.broadcasted_iota(jnp.int32, (LANES, LANES), 1)
    for side in range(sides):
        left = left_of(side)
        gap = (edge_in & (EDGE - 1)) - (edge_out & (EDGE - 1)) + EDGE - 2 * EDGE * left
        near = (slot_of(edge_in, left) == slot_of(edge_out, 1 - left)) & (jnp.abs(gap) <= HALF_RG)
        diag[side] = near.astype(F32).astype(BF16)

    line_out = lax.broadcasted_iota(jnp.int32, (lines, height), 0)
    row = lax.broadcasted_iota(jnp.int32, (lines, height), 1)
    line_in = row - jnp.where(row >= lines, az * height, 0)
    pick[...] = (jnp.abs(line_in - line_out) <= HALF_AZ).astype(F32).astype(BF16)

    def line_sums(rows):
        return jnp.dot(pick[...], rows, preferred_element_type=F32)

    def column_sums(rows):
        return jnp.dot(jnp.concatenate(rows, axis=0), band[...], preferred_element_type=F32)

    def halves(x):
        hi = x.astype(BF16)
        return hi, (x - hi.astype(F32)).astype(BF16)

    def part(e, i):
        return jnp.concatenate([tiles[e, i, b] for b in frame], axis=1)

    def twice():
        return jnp.concatenate([pick[...]] * 2, axis=1)

    lane = lax.broadcasted_iota(jnp.int32, (lines, LANES), 1)

    def with_edges(x, read, slot):
        out = [x[:, b * LANES:(b + 1) * LANES] for b in range(BLOCKS)]
        for side in range(sides):
            y = read(side)
            y = pltpu.roll(y, LANES - EDGE * slot, axis=1) if slot else y
            mine = slot_of(lane, 1 - left_of(side)) == 0
            out[side * (BLOCKS - 1)] += jnp.where(mine, y, 0.0)
        return jnp.concatenate(out, axis=1)

    def put(ref, value):
        for b in range(BLOCKS):
            if sides == 1:
                ref[:, pl.ds(pl.multiple_of(frame[b] * LANES, LANES), LANES)] = value[:, b * LANES:(b + 1) * LANES]
            else:
                ref[:, b * LANES:(b + 1) * LANES] = value[:, b * LANES:(b + 1) * LANES]

    def edges_of(late):
        early, tasks = [], []

        def power_task(side):
            box = []

            def first():
                a0 = edges[late, side, 0].astype(F32)
                a1 = edges[late, side, 1].astype(F32)
                z = jnp.dot(twice(), jnp.concatenate(halves(a0 * a0 + a1 * a1), axis=0), preferred_element_type=F32)
                box.extend(halves(z))

            def second():
                y = jnp.dot(jnp.concatenate(box, axis=0), diag[side], preferred_element_type=F32)
                edge_power[late, side] = y[0:lines] + y[lines:]

            return first, second

        def cross_task(side, group):
            box = []

            def first():
                a0, a1 = edges[0, side, 0], edges[0, side, 1]
                for lag in group:
                    b = [edges[late, side, i] for i in range(PARTS)]
                    if lag < LAG_MAX:
                        b = [pltpu.roll(x.astype(F32), LANES - EDGE * lag, axis=1).astype(BF16) for x in b]
                    z = line_sums(jnp.concatenate([a0 * b[0] + a1 * b[1], a1 * b[0] - a0 * b[1]], axis=1)).astype(BF16)
                    box.extend([z[:, 0:LANES], z[:, LANES:]])

            def second():
                y = jnp.dot(jnp.concatenate(box, axis=0), diag[side], preferred_element_type=F32)
                for i, lag in enumerate(group):
                    for part in range(PARTS):
                        at = (2 * i + part) * lines
                        edge_cross[late, side, lag - 1, part] = y[at:at + lines]

            return first, second

        for side in range(sides):
            early.append(power_task(side))
            lags_here = list(range(1, LAG_MAX + late))
            for start in range(0, len(lags_here), 4):
                tasks.append(cross_task(side, lags_here[start:start + 4]))
        return {"P": early, "Q": tasks}

    def powers_of(e):
        box = []

        def first():
            a0 = part(e, 0).astype(F32)
            a1 = part(e, 1).astype(F32)
            p = a0 * a0 + a1 * a1
            z = jnp.dot(twice(), jnp.concatenate(halves(p), axis=0), preferred_element_type=F32)
            box.extend(halves(z))
            box.append(p[0:lines] if e < dates else None)

        def second():
            y = column_sums(box[0:2])
            y = with_edges(y[0:lines] + y[lines:], lambda side: edge_power[e // dates, side], e % dates)
            m = y * (1.0 / LOOKS) + EPS
            r = 1.0 / m
            put(logs.at[e], jnp.log(m))
            inv[e] = r * (1.0 / LOOKS)
            if e < dates:
                mean[e] = m
                term = box[2] * r
                if e == 0:
                    acc[...] = term
                else:
                    acc[...] += term

        return [(first, second)]

    def pairs_of(e):
        tasks = []
        first, last = (0, e) if e < dates else (e - dates, dates)
        for start in range(first, last, BATCH):
            tasks.append(pair_task(e, range(start, min(start + BATCH, last))))
        return tasks

    def pair_task(e, group):
        box = []

        def first():
            b0, b1 = part(e, 0), part(e, 1)
            for d in group:
                a0, a1 = part(d, 0), part(d, 1)
                z = line_sums(jnp.concatenate([a0 * b0 + a1 * b1, a1 * b0 - a0 * b1], axis=1)).astype(BF16)
                box.extend([z[:, 0:cols], z[:, cols:]])

        def second():
            y = column_sums(box)
            for i, d in enumerate(group):
                sr = y[2 * i * lines:(2 * i + 1) * lines]
                si = y[(2 * i + 1) * lines:(2 * i + 2) * lines]
                lag = e - d
                sr = with_edges(sr, lambda side: edge_cross[e // dates, side, lag - 1, 0], d)
                si = with_edges(si, lambda side: edge_cross[e // dates, side, lag - 1, 1], d)
                put(coh.at[e, lag - 1], ((sr * sr + si * si) * (inv[d] * inv[e])).astype(BF16))

        return first, second

    def run_tasks(tasks):
        late = []
        for first, second in tasks:
            first()
            late.append(second)
            if len(late) > DEPTH:
                late.pop(0)()
        for second in late:
            second()

    def chain(way, to):
        return pltpu.make_async_remote_copy(
            src_ref=chain_out.at[way], dst_ref=chain_in.at[way],
            send_sem=c_send.at[way], recv_sem=c_recv.at[way],
            device_id={"date": to}, device_id_type=pl.DeviceIdType.MESH)

    def up_step(first):
        if not first:
            chain(0, date + 1).wait_recv()

        @pl.when(has_next)
        def _():
            s = acc[...] if first else acc[...] + chain_in[0].astype(F32)
            chain_out[0] = s.astype(BF16)
            chain(0, date + 1).start()

    def down_step(first):
        if not first:
            chain(1, date - 1).wait_recv()

        @pl.when(has_prev)
        def _():
            s = acc[...] if first else acc[...] + chain_in[1].astype(F32)
            chain_out[1] = s.astype(BF16)
            chain(1, date - 1).start()

    def chain_point(k, last):
        if last:
            pl.when(date >= k)(lambda: up_step(False))
            pl.when(date <= dates_axis - 1 - k)(lambda: down_step(False))
        else:
            pl.when(date == dates_axis - 1 - k)(lambda: down_step(k == 0))
            pl.when(date == k)(lambda: up_step(k == 0))

    def filtered():
        lag_copy.wait()
        up = jnp.where(has_prev, chain_in[0].astype(F32), 0.0)
        down = jnp.where(has_next, chain_in[1].astype(F32), 0.0)
        total = (acc[...] + up + down) * (1.0 / float(dates * dates_axis))
        for d in range(dates):
            put(queg.at[d], mean[d] * total)

    @pl.when(date == 0)
    def _():
        chain_in[0] = jnp.zeros((lines, cols), BF16)

    @pl.when(date == dates_axis - 1)
    def _():
        chain_in[1] = jnp.zeros((lines, cols), BF16)

    def z_wait(piece):
        for copy in z_copies(piece, date - 1):
            copy.wait_recv()

    def next_step(kind, i):
        if kind == "U":
            z_wait("p0")
        elif kind == "B":
            z_wait("b%d" % i)
            for copy in a_copies(i):
                copy.start()
        elif kind == "V":
            for copy in a_copies(i):
                copy.wait_recv()
        elif kind == "F":
            z_wait("f%d" % i)

    for copy in own_rows:
        copy.wait_recv()
    for g in range(groups):
        pack(g, 1)
    more = {}
    points = sum(word[0] == "K" for word in ORDER)
    todo = [(word[0], word[1:]) for word in ORDER]
    while todo:
        kind, i = todo.pop(0)
        if kind == "S":
            run = [i]
            while todo and todo[0][0] == "S":
                run.append(todo.pop(0)[1])
            send(run)
        elif kind == "T":
            filtered()
        elif kind == "X":
            for g in range(groups):
                x_wait(g)
            unpack(0)
            more = edges_of(0)
        elif kind in "PQ":
            tasks = more.pop(kind, []) + (powers_of if kind == "P" else pairs_of)(int(i))
            while todo and todo[0][0] in "PQ":
                kind, i = todo.pop(0)
                tasks += more.pop(kind, []) + (powers_of if kind == "P" else pairs_of)(int(i))
            run_tasks(tasks)
        elif kind == "K":
            if int(i) < dates_axis:
                chain_point(int(i), int(i) == points - 1)
        else:
            run = [(kind, int(i))]
            while todo and todo[0][0] in "BUVF":
                run.append((todo[0][0], int(todo.pop(0)[1])))

            @pl.when(has_next)
            def _():
                for step in run:
                    next_step(*step)
            if "U" in [step[0] for step in run]:
                unpack(1)
                more = edges_of(1)

    for copy in own_rows:
        copy.wait_send()
    for g in range(groups):
        for tail in range(2):
            x_each(g, tail, lambda c: c.wait_send())

    @pl.when(has_next)
    def _():
        for g in range(groups):
            for copy in a_copies(g):
                copy.wait_send()
        chain(0, date + 1).wait_send()

    @pl.when(has_prev)
    def _():
        for word in FIRST + [w for w in ORDER if w[0] == "S"]:
            for copy in z_copies(word[1:], date - 1):
                copy.wait_send()
        chain(1, date - 1).wait_send()


def pick_kernel(sizes, lags_in, coh, logs, queg, coh_out, log_out, queg_out,
                lags, zero, ratio, lag_sem, coh_sem, log_sem, queg_sem):
    dates, slots, lines, cols = sizes
    lag_copy = pltpu.make_async_copy(lags_in, lags, lag_sem)
    lag_copy.start()
    queg_copy = pltpu.make_async_copy(queg, queg_out, queg_sem)
    queg_copy.start()
    zero[...] = jnp.zeros((lines, cols), BF16)
    lag_copy.wait()

    def start(d, carry):
        for s in range(slots):
            lag = lags[d, s]

            @pl.when(lag > 0)
            def _():
                pltpu.make_async_copy(coh.at[d + lag, lag - 1], coh_out.at[d, s], coh_sem).start()

            @pl.when(lag <= 0)
            def _():
                pltpu.make_async_copy(zero, coh_out.at[d, s], coh_sem).start()
        return carry

    lax.fori_loop(0, dates, start, 0)

    def each(d, carry):
        for s in range(slots):
            lag = lags[d, s]
            there = d + jnp.maximum(lag, 0)
            keep = jnp.broadcast_to(lag > 0, (lines, cols))
            ratio[d, s] = jnp.where(keep, logs[d] - logs[there], 0.0).astype(BF16)
        pltpu.make_async_copy(ratio.at[d], log_out.at[d], log_sem).start()
        return carry

    lax.fori_loop(0, dates, each, 0)
    pltpu.make_async_copy(ratio, coh_out, coh_sem).wait()
    pltpu.make_async_copy(ratio, log_out, log_sem).wait()
    queg_copy.wait()


def solution(mesh):
    dates_axis, rng_axis, az_axis = mesh.shape["date"], mesh.shape["rng"], mesh.shape["az"]
    assert az_axis == 2 and rng_axis > 1
    sides = 1 if rng_axis == 2 else 2

    def on_device(slc, lags):
        dates, parts, lines, cols = slc.shape
        slots = lags.shape[1]
        assert cols == BLOCKS * LANES and dates == LAG_MAX and parts == PARTS and dates == 2 * GROUP
        groups = dates // GROUP
        pieces = 1 + dates + groups
        held = 4 * lines * cols * (LAG_MAX * dates + 3 * dates) + 4 * 8 * LANES
        height = lines + ROWS
        inside = pl.BlockSpec(memory_space=pltpu.VMEM)
        anywhere = pl.BlockSpec(memory_space=pltpu.HBM)
        field = (lines, cols)
        dma = pltpu.SemaphoreType.DMA
        coh, logs, queg, lags = pl.pallas_call(
            functools.partial(gather_kernel, (dates_axis, rng_axis, dates, lines, cols)),
            out_shape=[
                jax.ShapeDtypeStruct((2 * dates, LAG_MAX, *field), BF16),
                jax.ShapeDtypeStruct((2 * dates, *field), F32),
                jax.ShapeDtypeStruct((dates, *field), F32),
                jax.ShapeDtypeStruct(lags.shape, lags.dtype),
            ],
            in_specs=[anywhere] * 2,
            out_specs=[inside] * 4,
            scratch_shapes=[
                pltpu.VMEM((2 * dates, parts, BLOCKS, height, LANES), BF16),
                pltpu.VMEM((groups, sides, height, LANES), BF16),
                pltpu.VMEM((2, groups, sides, height, LANES), BF16),
                pltpu.VMEM((2, sides, parts, height, LANES), BF16),
                pltpu.VMEM((2, sides, lines, LANES), F32),
                pltpu.VMEM((2, sides, LAG_MAX, parts, lines, LANES), F32),
                pltpu.VMEM((cols, cols), BF16),
                pltpu.VMEM((sides, LANES, LANES), BF16),
                pltpu.VMEM((lines, height), BF16),
                pltpu.VMEM((2 * dates, *field), F32),
                pltpu.VMEM((dates, *field), F32),
                pltpu.VMEM(field, F32),
                pltpu.VMEM((2, *field), BF16),
                pltpu.VMEM((2, *field), BF16),
                dma((BLOCKS,)), dma, dma((pieces, BLOCKS)), dma((pieces, BLOCKS)),
                dma((1 + groups, BLOCKS)), dma((1 + groups, BLOCKS)),
                dma((sides, groups, 2)), dma((sides, groups, 2)),
                dma((2,)), dma((2,)),
            ],
            compiler_params=pltpu.CompilerParams(collective_id=0, has_side_effects=True, vmem_limit_bytes=VMEM_BYTES - SPARE - held),
            name="gather",
        )(pltpu.with_memory_space_constraint(slc, pltpu.HBM), pltpu.with_memory_space_constraint(lags, pltpu.HBM))
        return pl.pallas_call(
            functools.partial(pick_kernel, (dates, slots, lines, cols)),
            out_shape=[
                jax.ShapeDtypeStruct((dates, slots, *field), BF16),
                jax.ShapeDtypeStruct((dates, slots, *field), BF16),
                jax.ShapeDtypeStruct((dates, *field), F32),
            ],
            in_specs=[inside] * 4,
            out_specs=[anywhere] * 3,
            scratch_shapes=[
                pltpu.SMEM((dates, slots), jnp.int32),
                pltpu.VMEM(field, BF16),
                pltpu.VMEM((dates, slots, *field), BF16),
                dma, dma, dma, dma,
            ],
            compiler_params=pltpu.CompilerParams(vmem_limit_bytes=16 * 2 ** 20),
            name="pick",
        )(lags, coh, logs, queg)

    return jax.shard_map(
        on_device,
        mesh=mesh,
        in_specs=(P(("slab", "date"), None, "az", "rng"), P("date", None)),
        out_specs=(
            P(("slab", "date"), None, "az", "rng"),
            P(("slab", "date"), None, "az", "rng"),
            P(("slab", "date"), "az", "rng"),
        ),
        check_vma=False,
    )
```

```python
import functools

import jax
import jax.numpy as jnp
from jax import lax
from jax.experimental import pallas as pl
from jax.experimental.pallas import tpu as pltpu
from jax.sharding import PartitionSpec as P

HALF_AZ = 2
HALF_RG = 10
LAG_MAX = 8
EPS = 1e-05
LOOKS = float((2 * HALF_AZ + 1) * (2 * HALF_RG + 1))

LANES = 128
ROWS = 16
EDGE = 16
PARTS = 2
BLOCKS = 2
LP = True
DEPTH = 1
GROUP = LANES // (EDGE * PARTS)
BATCH = 4
VMEM_BYTES = 67043328
SPARE = 16 * 2 ** 20
F32 = jnp.float32
BF16 = jnp.bfloat16

ORDER = [
    "X0 Sp0 P0 P1",
    "P2 P3 P4 P5",
    "P6 P7 B0 K0",
    "Sf2 Sf3 Sb1 Q1",
    "Q2 Q3 Q4 Q5",
    "Q6 Q7 V0 U0",
    "F0 P8 K1 Sf4",
    "Sf5 Sf6 Sf7 Q8",
    "F1 P9 Q9 F2",
    "P10 Q10 F3 P11",
    "Q11 K2 B1 V1",
    "F4 P12 Q12 F5",
    "P13 Q13 F6 P14",
    "Q14 F7 P15 Q15",
    "K3 T",
]
ORDER = [word for words in ORDER for word in words.split()]
FIRST = ["Sb0", "Sf0", "Sf1"]


def gather_kernel(sizes, slc, lags_in, coh, logs, mean, total, lags,
                  tiles, packs_out, packs_in, edges, edge_power, edge_cross, band, diag, pick, inv, acc, chain_out, chain_in,
                  own_sem, lag_sem, z_send, z_recv, a_send, a_recv, x_send, x_recv,
                  c_send, c_recv):
    dates_axis, rng_axis, dates, lines, cols = sizes
    sides = 1 if rng_axis == 2 else 2
    groups = dates // GROUP
    date = lax.axis_index("date")
    rng = lax.axis_index("rng")
    az = lax.axis_index("az")
    has_next = date < dates_axis - 1
    has_prev = date > 0
    has_right = rng < rng_axis - 1
    has_left = rng > 0
    peer = 1 - az
    height = lines + ROWS

    barrier = pltpu.get_barrier_semaphore()

    def greet(where):
        pl.semaphore_signal(barrier, inc=1, device_id=where, device_id_type=pl.DeviceIdType.MESH)

    greet({"az": peer})
    pl.when(has_next)(lambda: greet({"date": date + 1}))
    pl.when(has_left)(lambda: greet({"rng": rng - 1}))
    pl.when(has_right)(lambda: greet({"rng": rng + 1}))

    def block_of(b):
        return pl.ds(b * LANES if isinstance(b, int) else pl.multiple_of(b * LANES, LANES), LANES)

    own = [
        pltpu.make_async_copy(
            slc.at[:, :, :, block_of(b)], tiles.at[pl.ds(0, dates), :, b, pl.ds(0, lines), :], own_sem.at[b])
        for b in range(BLOCKS)]
    for copy in own:
        copy.start()
    lag_copy = pltpu.make_async_copy(lags_in, lags, lag_sem)
    lag_copy.start()

    border = pl.multiple_of((1 - az) * (lines - ROWS), ROWS)
    rest = pl.multiple_of(az * ROWS, ROWS)

    def z_copies(piece, to):
        kind, i = piece[0], int(piece[1:])
        if kind == "p":
            return [pltpu.make_async_remote_copy(
                src_ref=packs_in.at[0], dst_ref=packs_in.at[1],
                send_sem=z_send.at[0, 0], recv_sem=z_recv.at[0, 0],
                device_id={"date": to}, device_id_type=pl.DeviceIdType.MESH)]
        if kind == "b":
            first, count, row, rows, k = i * GROUP, GROUP, border, ROWS, 1 + i
        else:
            first, count, row, rows, k = i, 1, rest, lines - ROWS, 1 + groups + i
        return [
            pltpu.make_async_remote_copy(
                src_ref=slc.at[pl.ds(first, count), :, pl.ds(row, rows), block_of(b)],
                dst_ref=tiles.at[pl.ds(dates + first, count), :, b, pl.ds(row, rows), :],
                send_sem=z_send.at[k, b], recv_sem=z_recv.at[k, b],
                device_id={"date": to}, device_id_type=pl.DeviceIdType.MESH)
            for b in range(BLOCKS)]

    own_rows = [
        pltpu.make_async_remote_copy(
            src_ref=slc.at[:, :, pl.ds(border, ROWS), block_of(b)],
            dst_ref=tiles.at[pl.ds(0, dates), :, b, pl.ds(lines, ROWS), :],
            send_sem=a_send.at[0, b], recv_sem=a_recv.at[0, b],
            device_id={"az": peer}, device_id_type=pl.DeviceIdType.MESH)
        for b in range(BLOCKS)]

    def a_copies(g):
        where = pl.ds(dates + g * GROUP, GROUP)
        return [
            pltpu.make_async_remote_copy(
                src_ref=tiles.at[where, :, b, pl.ds(border, ROWS), :],
                dst_ref=tiles.at[where, :, b, pl.ds(lines, ROWS), :],
                send_sem=a_send.at[1 + g, b], recv_sem=a_recv.at[1 + g, b],
                device_id={"az": peer}, device_id_type=pl.DeviceIdType.MESH)
            for b in range(BLOCKS)]

    def x_copy(g, tail, side, to):
        rows = pl.ds(lines, ROWS) if tail else pl.ds(0, lines)
        return pltpu.make_async_remote_copy(
            src_ref=packs_out.at[g, side, rows, :],
            dst_ref=packs_in.at[0, g, side, rows, :],
            send_sem=x_send.at[side, g, tail], recv_sem=x_recv.at[side, g, tail],
            device_id={"rng": to}, device_id_type=pl.DeviceIdType.MESH)

    def x_each(g, tail, act):
        if sides == 1:
            act(x_copy(g, tail, 0, 1 - rng))
        else:
            pl.when(has_right)(lambda: act(x_copy(g, tail, 0, rng + 1)))
            pl.when(has_left)(lambda: act(x_copy(g, tail, 1, rng - 1)))

    def x_wait(g):
        for tail in range(2):
            if sides == 1:
                x_copy(g, tail, 0, 1 - rng).wait_recv()
            else:
                pl.when(has_left)(lambda: x_copy(g, tail, 0, rng - 1).wait_recv())
                pl.when(has_right)(lambda: x_copy(g, tail, 1, rng + 1).wait_recv())

    def left_of(side):
        return rng if sides == 1 else 1 - side

    def slot_of(lane, left):
        return lax.shift_right_logical((lane + EDGE * left) & (LANES - 1), EDGE.bit_length() - 1)

    def pack(g, tail):
        first, rows = (lines, ROWS) if tail else (0, lines)
        lane = lax.broadcasted_iota(jnp.int32, (rows, LANES), 1)
        for side in range(sides):
            high = 1 - rng if sides == 1 else 1 - side
            block = 1 - rng if sides == 1 else (1 - side) * (BLOCKS - 1)
            slot = slot_of(lane, high)
            out = None
            for s in range(GROUP * PARTS):
                x = tiles[g * GROUP + s % GROUP, s // GROUP, block, first:first + rows, :].astype(F32)
                out = x if s == 0 else jnp.where(slot == s, pltpu.roll(x, EDGE * s, axis=1), out)
            packs_out[g, side, first:first + rows] = out.astype(BF16)
        x_each(g, tail, lambda c: c.start())

    def unpack(late):
        lane = lax.broadcasted_iota(jnp.int32, (height, LANES), 1)
        for side in range(sides):
            lower = slot_of(lane, left_of(side)) < GROUP
            x = packs_in[late, 0, side].astype(F32)
            y = packs_in[late, 1, side].astype(F32)
            edges[late, side, 0] = jnp.where(lower, x, pltpu.roll(y, LANES // 2, axis=1)).astype(BF16)
            edges[late, side, 1] = jnp.where(lower, pltpu.roll(x, LANES // 2, axis=1), y).astype(BF16)

    if sides == 2:
        @pl.when(rng == 0)
        def _():
            packs_in[0, :, 0] = jnp.zeros((groups, height, LANES), BF16)

        @pl.when(rng == rng_axis - 1)
        def _():
            packs_in[0, :, 1] = jnp.zeros((groups, height, LANES), BF16)

    peers = 1
    for cond in (has_prev, has_left, has_right):
        peers = peers + cond.astype(jnp.int32)
    pl.semaphore_wait(barrier, peers)

    def send(pieces):
        @pl.when(has_prev)
        def _():
            for piece in pieces:
                for copy in z_copies(piece, date - 1):
                    copy.start()

    send([word[1:] for word in FIRST])
    for copy in own_rows:
        copy.start()
    for copy in own:
        copy.wait()
    for g in range(groups):
        pack(g, 0)

    @pl.when(date == dates_axis - 1)
    def _():
        tiles[dates:] = jnp.zeros((dates, PARTS, BLOCKS, height, LANES), BF16)
        packs_in[1] = jnp.zeros((groups, sides, height, LANES), BF16)

    frame = (1 - rng, rng) if sides == 1 else tuple(range(BLOCKS))

    def column_of(index):
        return jnp.where(index < LANES, LANES * frame[0], LANES * (frame[1] - 1)) + index

    col_out = column_of(lax.broadcasted_iota(jnp.int32, (cols, cols), 1))
    col_in = column_of(lax.broadcasted_iota(jnp.int32, (cols, cols), 0))
    band[...] = (jnp.abs(col_in - col_out) <= HALF_RG).astype(F32).astype(BF16)
    edge_in = lax.broadcasted_iota(jnp.int32, (LANES, LANES), 0)
    edge_out = lax.broadcasted_iota(jnp.int32, (LANES, LANES), 1)
    for side in range(sides):
        left = left_of(side)
        gap = (edge_in & (EDGE - 1)) - (edge_out & (EDGE - 1)) + EDGE - 2 * EDGE * left
        near = (slot_of(edge_in, left) == slot_of(edge_out, 1 - left)) & (jnp.abs(gap) <= HALF_RG)
        diag[side] = near.astype(F32).astype(BF16)

    line_out = lax.broadcasted_iota(jnp.int32, (lines, height), 0)
    row = lax.broadcasted_iota(jnp.int32, (lines, height), 1)
    line_in = row - jnp.where(row >= lines, az * height, 0)
    pick[...] = (jnp.abs(line_in - line_out) <= HALF_AZ).astype(F32).astype(BF16)

    def line_sums(rows):
        return jnp.dot(pick[...], rows, preferred_element_type=F32)

    def column_sums(rows):
        return jnp.dot(jnp.concatenate(rows, axis=0), band[...], preferred_element_type=F32)

    def halves(x):
        hi = x.astype(BF16)
        return hi, (x - hi.astype(F32)).astype(BF16)

    def part(e, i):
        return jnp.concatenate([tiles[e, i, b] for b in frame], axis=1)

    def twice():
        return jnp.concatenate([pick[...]] * 2, axis=1)

    lane = lax.broadcasted_iota(jnp.int32, (lines, LANES), 1)

    def with_edges(x, read, slot):
        out = [x[:, b * LANES:(b + 1) * LANES] for b in range(BLOCKS)]
        for side in range(sides):
            y = read(side)
            y = pltpu.roll(y, LANES - EDGE * slot, axis=1) if slot else y
            mine = slot_of(lane, 1 - left_of(side)) == 0
            out[side * (BLOCKS - 1)] += jnp.where(mine, y, 0.0)
        return jnp.concatenate(out, axis=1)

    def put(ref, value):
        for b in range(BLOCKS):
            if sides == 1:
                ref[:, pl.ds(pl.multiple_of(frame[b] * LANES, LANES), LANES)] = value[:, b * LANES:(b + 1) * LANES]
            else:
                ref[:, b * LANES:(b + 1) * LANES] = value[:, b * LANES:(b + 1) * LANES]

    def edges_of(late):
        early, tasks = [], []

        def power_task(side):
            box = []

            def first():
                a0 = edges[late, side, 0].astype(F32)
                a1 = edges[late, side, 1].astype(F32)
                z = jnp.dot(twice(), jnp.concatenate(halves(a0 * a0 + a1 * a1), axis=0), preferred_element_type=F32)
                box.extend(halves(z))

            def second():
                y = jnp.dot(jnp.concatenate(box, axis=0), diag[side], preferred_element_type=F32)
                edge_power[late, side] = y[0:lines] + y[lines:]

            return first, second

        def cross_task(side, group):
            box = []

            def first():
                a0, a1 = edges[0, side, 0], edges[0, side, 1]
                for lag in group:
                    b = [edges[late, side, i] for i in range(PARTS)]
                    if lag < LAG_MAX:
                        b = [pltpu.roll(x.astype(F32), LANES - EDGE * lag, axis=1).astype(BF16) for x in b]
                    z = line_sums(jnp.concatenate([a0 * b[0] + a1 * b[1], a1 * b[0] - a0 * b[1]], axis=1)).astype(BF16)
                    box.extend([z[:, 0:LANES], z[:, LANES:]])

            def second():
                y = jnp.dot(jnp.concatenate(box, axis=0), diag[side], preferred_element_type=F32)
                for i, lag in enumerate(group):
                    for part in range(PARTS):
                        at = (2 * i + part) * lines
                        edge_cross[late, side, lag - 1, part] = y[at:at + lines]

            return first, second

        for side in range(sides):
            early.append(power_task(side))
            lags_here = list(range(1, LAG_MAX + late))
            for start in range(0, len(lags_here), 4):
                tasks.append(cross_task(side, lags_here[start:start + 4]))
        return {"P": early, "Q": tasks}

    def powers_of(e):
        box = []

        def first():
            a0 = part(e, 0).astype(F32)
            a1 = part(e, 1).astype(F32)
            p = a0 * a0 + a1 * a1
            z = jnp.dot(twice(), jnp.concatenate(halves(p), axis=0), preferred_element_type=F32)
            box.extend(halves(z))
            box.append(p[0:lines] if e < dates else None)

        def second():
            y = column_sums(box[0:2])
            y = with_edges(y[0:lines] + y[lines:], lambda side: edge_power[e // dates, side], e % dates)
            m = y * (1.0 / LOOKS) + EPS
            r = 1.0 / m
            put(logs.at[e], jnp.log(m))
            inv[e] = r * (1.0 / LOOKS)
            if e < dates:
                put(mean.at[e], m)
                term = box[2] * r
                if e == 0:
                    acc[...] = term
                else:
                    acc[...] += term

        return [(first, second)]

    def pairs_of(e):
        tasks = []
        first, last = (0, e) if e < dates else (e - dates, dates)
        for start in range(first, last, BATCH):
            tasks.append(pair_task(e, range(start, min(start + BATCH, last))))
        return tasks

    def pair_task(e, group):
        box = []

        def first():
            b0, b1 = part(e, 0), part(e, 1)
            for d in group:
                a0, a1 = part(d, 0), part(d, 1)
                z = line_sums(jnp.concatenate([a0 * b0 + a1 * b1, a1 * b0 - a0 * b1], axis=1)).astype(BF16)
                box.extend([z[:, 0:cols], z[:, cols:]])

        def second():
            y = column_sums(box)
            for i, d in enumerate(group):
                sr = y[2 * i * lines:(2 * i + 1) * lines]
                si = y[(2 * i + 1) * lines:(2 * i + 2) * lines]
                lag = e - d
                sr = with_edges(sr, lambda side: edge_cross[e // dates, side, lag - 1, 0], d)
                si = with_edges(si, lambda side: edge_cross[e // dates, side, lag - 1, 1], d)
                put(coh.at[e, lag - 1], ((sr * sr + si * si) * (inv[d] * inv[e])).astype(BF16))

        return first, second

    def run_tasks(tasks):
        late = []
        for first, second in tasks:
            first()
            late.append(second)
            if len(late) > DEPTH:
                late.pop(0)()
        for second in late:
            second()

    def chain(way, to):
        return pltpu.make_async_remote_copy(
            src_ref=chain_out.at[way], dst_ref=chain_in.at[way],
            send_sem=c_send.at[way], recv_sem=c_recv.at[way],
            device_id={"date": to}, device_id_type=pl.DeviceIdType.MESH)

    def up_step(first):
        if not first:
            chain(0, date + 1).wait_recv()

        @pl.when(has_next)
        def _():
            s = acc[...] if first else acc[...] + chain_in[0].astype(F32)
            chain_out[0] = s.astype(BF16)
            chain(0, date + 1).start()

    def down_step(first):
        if not first:
            chain(1, date - 1).wait_recv()

        @pl.when(has_prev)
        def _():
            s = acc[...] if first else acc[...] + chain_in[1].astype(F32)
            chain_out[1] = s.astype(BF16)
            chain(1, date - 1).start()

    def chain_point(k, last):
        if last:
            pl.when(date >= k)(lambda: up_step(False))
            pl.when(date <= dates_axis - 1 - k)(lambda: down_step(False))
        else:
            pl.when(date == dates_axis - 1 - k)(lambda: down_step(k == 0))
            pl.when(date == k)(lambda: up_step(k == 0))

    def filtered():
        lag_copy.wait()
        up = jnp.where(has_prev, chain_in[0].astype(F32), 0.0)
        down = jnp.where(has_next, chain_in[1].astype(F32), 0.0)
        put(total, (acc[...] + up + down) * (1.0 / float(dates * dates_axis)))

    @pl.when(date == 0)
    def _():
        chain_in[0] = jnp.zeros((lines, cols), BF16)

    @pl.when(date == dates_axis - 1)
    def _():
        chain_in[1] = jnp.zeros((lines, cols), BF16)

    def z_wait(piece):
        for copy in z_copies(piece, date - 1):
            copy.wait_recv()

    def next_step(kind, i):
        if kind == "U":
            z_wait("p0")
        elif kind == "B":
            z_wait("b%d" % i)
            for copy in a_copies(i):
                copy.start()
        elif kind == "V":
            for copy in a_copies(i):
                copy.wait_recv()
        elif kind == "F":
            z_wait("f%d" % i)

    for copy in own_rows:
        copy.wait_recv()
    for g in range(groups):
        pack(g, 1)
    more = {}
    points = sum(word[0] == "K" for word in ORDER)
    todo = [(word[0], word[1:]) for word in ORDER]
    while todo:
        kind, i = todo.pop(0)
        if kind == "S":
            run = [i]
            while todo and todo[0][0] == "S":
                run.append(todo.pop(0)[1])
            send(run)
        elif kind == "T":
            filtered()
        elif kind == "X":
            for g in range(groups):
                x_wait(g)
            unpack(0)
            more = edges_of(0)
        elif kind in "PQ":
            tasks = more.pop(kind, []) + (powers_of if kind == "P" else pairs_of)(int(i))
            while todo and todo[0][0] in "PQ":
                kind, i = todo.pop(0)
                tasks += more.pop(kind, []) + (powers_of if kind == "P" else pairs_of)(int(i))
            run_tasks(tasks)
        elif kind == "K":
            if int(i) < dates_axis:
                chain_point(int(i), int(i) == points - 1)
        else:
            run = [(kind, int(i))]
            while todo and todo[0][0] in "BUVF":
                run.append((todo[0][0], int(todo.pop(0)[1])))

            @pl.when(has_next)
            def _():
                for step in run:
                    next_step(*step)
            if "U" in [step[0] for step in run]:
                unpack(1)
                more = edges_of(1)

    for copy in own_rows:
        copy.wait_send()
    for g in range(groups):
        for tail in range(2):
            x_each(g, tail, lambda c: c.wait_send())

    @pl.when(has_next)
    def _():
        for g in range(groups):
            for copy in a_copies(g):
                copy.wait_send()
        chain(0, date + 1).wait_send()

    @pl.when(has_prev)
    def _():
        for word in FIRST + [w for w in ORDER if w[0] == "S"]:
            for copy in z_copies(word[1:], date - 1):
                copy.wait_send()
        chain(1, date - 1).wait_send()


def pick_kernel(sizes, lags_in, coh, logs, mean, total, coh_out, log_out, queg_out,
                lags, zero, ratio, queg, lag_sem, coh_sem, log_sem, queg_sem):
    dates, slots, lines, cols = sizes
    lag_copy = pltpu.make_async_copy(lags_in, lags, lag_sem)
    lag_copy.start()
    for d in range(dates):
        queg[d] = mean[d] * total[...]
    queg_copy = pltpu.make_async_copy(queg, queg_out, queg_sem)
    queg_copy.start()
    zero[...] = jnp.zeros((lines, cols), BF16)
    lag_copy.wait()

    def start(d, carry):
        for s in range(slots):
            lag = lags[d, s]

            @pl.when(lag > 0)
            def _():
                pltpu.make_async_copy(coh.at[d + lag, lag - 1], coh_out.at[d, s], coh_sem).start()

            @pl.when(lag <= 0)
            def _():
                pltpu.make_async_copy(zero, coh_out.at[d, s], coh_sem).start()
        return carry

    lax.fori_loop(0, dates, start, 0)

    def each(d, carry):
        for s in range(slots):
            lag = lags[d, s]
            there = d + jnp.maximum(lag, 0)
            keep = jnp.broadcast_to(lag > 0, (lines, cols))
            ratio[d, s] = jnp.where(keep, logs[d] - logs[there], 0.0).astype(BF16)
        pltpu.make_async_copy(ratio.at[d], log_out.at[d], log_sem).start()
        return carry

    lax.fori_loop(0, dates, each, 0)
    pltpu.make_async_copy(ratio, coh_out, coh_sem).wait()
    pltpu.make_async_copy(ratio, log_out, log_sem).wait()
    queg_copy.wait()


def solution(mesh):
    dates_axis, rng_axis, az_axis = mesh.shape["date"], mesh.shape["rng"], mesh.shape["az"]
    assert az_axis == 2 and rng_axis > 1
    sides = 1 if rng_axis == 2 else 2

    def on_device(slc, lags):
        dates, parts, lines, cols = slc.shape
        slots = lags.shape[1]
        assert cols == BLOCKS * LANES and dates == LAG_MAX and parts == PARTS and dates == 2 * GROUP
        groups = dates // GROUP
        pieces = 1 + dates + groups
        held = 4 * lines * cols * (LAG_MAX * dates + 3 * dates + 1) + 4 * 8 * LANES
        height = lines + ROWS
        inside = pl.BlockSpec(memory_space=pltpu.VMEM)
        anywhere = pl.BlockSpec(memory_space=pltpu.HBM)
        field = (lines, cols)
        dma = pltpu.SemaphoreType.DMA
        coh, logs, mean, total, lags = pl.pallas_call(
            functools.partial(gather_kernel, (dates_axis, rng_axis, dates, lines, cols)),
            out_shape=[
                jax.ShapeDtypeStruct((2 * dates, LAG_MAX, *field), BF16),
                jax.ShapeDtypeStruct((2 * dates, *field), F32),
                jax.ShapeDtypeStruct((dates, *field), F32),
                jax.ShapeDtypeStruct(field, F32),
                jax.ShapeDtypeStruct(lags.shape, lags.dtype),
            ],
            in_specs=[anywhere] * 2,
            out_specs=[inside] * 5,
            scratch_shapes=[
                pltpu.VMEM((2 * dates, parts, BLOCKS, height, LANES), BF16),
                pltpu.VMEM((groups, sides, height, LANES), BF16),
                pltpu.VMEM((2, groups, sides, height, LANES), BF16),
                pltpu.VMEM((2, sides, parts, height, LANES), BF16),
                pltpu.VMEM((2, sides, lines, LANES), F32),
                pltpu.VMEM((2, sides, LAG_MAX, parts, lines, LANES), F32),
                pltpu.VMEM((cols, cols), BF16),
                pltpu.VMEM((sides, LANES, LANES), BF16),
                pltpu.VMEM((lines, height), BF16),
                pltpu.VMEM((2 * dates, *field), F32),
                pltpu.VMEM(field, F32),
                pltpu.VMEM((2, *field), BF16),
                pltpu.VMEM((2, *field), BF16),
                dma((BLOCKS,)), dma, dma((pieces, BLOCKS)), dma((pieces, BLOCKS)),
                dma((1 + groups, BLOCKS)), dma((1 + groups, BLOCKS)),
                dma((sides, groups, 2)), dma((sides, groups, 2)),
                dma((2,)), dma((2,)),
            ],
            compiler_params=pltpu.CompilerParams(collective_id=0, has_side_effects=True, vmem_limit_bytes=VMEM_BYTES - SPARE - held),
            name="gather",
        )(pltpu.with_memory_space_constraint(slc, pltpu.HBM), pltpu.with_memory_space_constraint(lags, pltpu.HBM))
        return pl.pallas_call(
            functools.partial(pick_kernel, (dates, slots, lines, cols)),
            out_shape=[
                jax.ShapeDtypeStruct((dates, slots, *field), BF16),
                jax.ShapeDtypeStruct((dates, slots, *field), BF16),
                jax.ShapeDtypeStruct((dates, *field), F32),
            ],
            in_specs=[inside] * 5,
            out_specs=[anywhere] * 3,
            scratch_shapes=[
                pltpu.SMEM((dates, slots), jnp.int32),
                pltpu.VMEM(field, BF16),
                pltpu.VMEM((dates, slots, *field), BF16),
                pltpu.VMEM((dates, *field), F32),
                dma, dma, dma, dma,
            ],
            compiler_params=pltpu.CompilerParams(vmem_limit_bytes=16 * 2 ** 20),
            name="pick",
        )(lags, coh, logs, mean, total)

    return jax.shard_map(
        on_device,
        mesh=mesh,
        in_specs=(P(("slab", "date"), None, "az", "rng"), P("date", None)),
        out_specs=(
            P(("slab", "date"), None, "az", "rng"),
            P(("slab", "date"), None, "az", "rng"),
            P(("slab", "date"), "az", "rng"),
        ),
        check_vma=False,
    )
```

```python
import functools

import jax
import jax.numpy as jnp
from jax import lax
from jax.experimental import pallas as pl
from jax.experimental.pallas import tpu as pltpu
from jax.sharding import PartitionSpec as P

HALF_AZ = 2
HALF_RG = 10
LAG_MAX = 8
EPS = 1e-05
LOOKS = float((2 * HALF_AZ + 1) * (2 * HALF_RG + 1))

LANES = 128
ROWS = 16
EDGE = 16
PARTS = 2
BLOCKS = 2
LP = True
DEPTH = 1
GROUP = LANES // (EDGE * PARTS)
BATCH = 4
VMEM_BYTES = 67043328
SPARE = 16 * 2 ** 20
F32 = jnp.float32
BF16 = jnp.bfloat16

ORDER = [
    "X0 Sp0 P0 P1",
    "P2 P3 P4 P5",
    "P6 P7 B0 K0",
    "Sf2 Sf3 Sb1 Q1",
    "Q2 Q3 Q4 Q5",
    "Q6 Q7 V0 U0",
    "F0 P8 K1 Sf4",
    "Sf5 Sf6 Sf7 Q8",
    "F1 P9 Q9 F2",
    "P10 Q10 K2 F3",
    "P11 Q11 B1 V1",
    "F4 P12 Q12 F5",
    "P13 Q13 F6 P14",
    "Q14 F7 P15 Q15",
    "K3 T",
]
ORDER = [word for words in ORDER for word in words.split()]
FIRST = ["Sb0", "Sf0", "Sf1"]


def gather_kernel(sizes, slc, lags_in, coh, logs, mean, total, lags,
                  tiles, packs_out, packs_in, edges, edge_power, edge_cross, band, diag, pick, inv, acc, chain_out, chain_in,
                  own_sem, lag_sem, z_send, z_recv, a_send, a_recv, x_send, x_recv,
                  c_send, c_recv):
    dates_axis, rng_axis, dates, lines, cols = sizes
    sides = 1 if rng_axis == 2 else 2
    groups = dates // GROUP
    date = lax.axis_index("date")
    rng = lax.axis_index("rng")
    az = lax.axis_index("az")
    has_next = date < dates_axis - 1
    has_prev = date > 0
    has_right = rng < rng_axis - 1
    has_left = rng > 0
    peer = 1 - az
    height = lines + ROWS

    barrier = pltpu.get_barrier_semaphore()

    def greet(where):
        pl.semaphore_signal(barrier, inc=1, device_id=where, device_id_type=pl.DeviceIdType.MESH)

    greet({"az": peer})
    pl.when(has_next)(lambda: greet({"date": date + 1}))
    pl.when(has_left)(lambda: greet({"rng": rng - 1}))
    pl.when(has_right)(lambda: greet({"rng": rng + 1}))

    def block_of(b):
        return pl.ds(b * LANES if isinstance(b, int) else pl.multiple_of(b * LANES, LANES), LANES)

    own = [
        pltpu.make_async_copy(
            slc.at[:, :, :, block_of(b)], tiles.at[pl.ds(0, dates), :, b, pl.ds(0, lines), :], own_sem.at[b])
        for b in range(BLOCKS)]
    for copy in own:
        copy.start()
    lag_copy = pltpu.make_async_copy(lags_in, lags, lag_sem)
    lag_copy.start()

    border = pl.multiple_of((1 - az) * (lines - ROWS), ROWS)
    rest = pl.multiple_of(az * ROWS, ROWS)

    def z_copies(piece, to):
        kind, i = piece[0], int(piece[1:])
        if kind == "p":
            return [pltpu.make_async_remote_copy(
                src_ref=packs_in.at[0], dst_ref=packs_in.at[1],
                send_sem=z_send.at[0, 0], recv_sem=z_recv.at[0, 0],
                device_id={"date": to}, device_id_type=pl.DeviceIdType.MESH)]
        if kind == "b":
            first, count, row, rows, k = i * GROUP, GROUP, border, ROWS, 1 + i
        else:
            first, count, row, rows, k = i, 1, rest, lines - ROWS, 1 + groups + i
        return [
            pltpu.make_async_remote_copy(
                src_ref=slc.at[pl.ds(first, count), :, pl.ds(row, rows), block_of(b)],
                dst_ref=tiles.at[pl.ds(dates + first, count), :, b, pl.ds(row, rows), :],
                send_sem=z_send.at[k, b], recv_sem=z_recv.at[k, b],
                device_id={"date": to}, device_id_type=pl.DeviceIdType.MESH)
            for b in range(BLOCKS)]

    own_rows = [
        pltpu.make_async_remote_copy(
            src_ref=slc.at[:, :, pl.ds(border, ROWS), block_of(b)],
            dst_ref=tiles.at[pl.ds(0, dates), :, b, pl.ds(lines, ROWS), :],
            send_sem=a_send.at[0, b], recv_sem=a_recv.at[0, b],
            device_id={"az": peer}, device_id_type=pl.DeviceIdType.MESH)
        for b in range(BLOCKS)]

    def a_copies(g):
        where = pl.ds(dates + g * GROUP, GROUP)
        return [
            pltpu.make_async_remote_copy(
                src_ref=tiles.at[where, :, b, pl.ds(border, ROWS), :],
                dst_ref=tiles.at[where, :, b, pl.ds(lines, ROWS), :],
                send_sem=a_send.at[1 + g, b], recv_sem=a_recv.at[1 + g, b],
                device_id={"az": peer}, device_id_type=pl.DeviceIdType.MESH)
            for b in range(BLOCKS)]

    def x_copy(g, tail, side, to):
        rows = pl.ds(lines, ROWS) if tail else pl.ds(0, lines)
        return pltpu.make_async_remote_copy(
            src_ref=packs_out.at[g, side, rows, :],
            dst_ref=packs_in.at[0, g, side, rows, :],
            send_sem=x_send.at[side, g, tail], recv_sem=x_recv.at[side, g, tail],
            device_id={"rng": to}, device_id_type=pl.DeviceIdType.MESH)

    def x_each(g, tail, act):
        if sides == 1:
            act(x_copy(g, tail, 0, 1 - rng))
        else:
            pl.when(has_right)(lambda: act(x_copy(g, tail, 0, rng + 1)))
            pl.when(has_left)(lambda: act(x_copy(g, tail, 1, rng - 1)))

    def x_wait(g):
        for tail in range(2):
            if sides == 1:
                x_copy(g, tail, 0, 1 - rng).wait_recv()
            else:
                pl.when(has_left)(lambda: x_copy(g, tail, 0, rng - 1).wait_recv())
                pl.when(has_right)(lambda: x_copy(g, tail, 1, rng + 1).wait_recv())

    def left_of(side):
        return rng if sides == 1 else 1 - side

    def slot_of(lane, left):
        return lax.shift_right_logical((lane + EDGE * left) & (LANES - 1), EDGE.bit_length() - 1)

    def pack(g, tail):
        first, rows = (lines, ROWS) if tail else (0, lines)
        lane = lax.broadcasted_iota(jnp.int32, (rows, LANES), 1)
        for side in range(sides):
            high = 1 - rng if sides == 1 else 1 - side
            block = 1 - rng if sides == 1 else (1 - side) * (BLOCKS - 1)
            slot = slot_of(lane, high)
            out = None
            for s in range(GROUP * PARTS):
                x = tiles[g * GROUP + s % GROUP, s // GROUP, block, first:first + rows, :].astype(F32)
                out = x if s == 0 else jnp.where(slot == s, pltpu.roll(x, EDGE * s, axis=1), out)
            packs_out[g, side, first:first + rows] = out.astype(BF16)
        x_each(g, tail, lambda c: c.start())

    def unpack(late):
        lane = lax.broadcasted_iota(jnp.int32, (height, LANES), 1)
        for side in range(sides):
            lower = slot_of(lane, left_of(side)) < GROUP
            x = packs_in[late, 0, side].astype(F32)
            y = packs_in[late, 1, side].astype(F32)
            edges[late, side, 0] = jnp.where(lower, x, pltpu.roll(y, LANES // 2, axis=1)).astype(BF16)
            edges[late, side, 1] = jnp.where(lower, pltpu.roll(x, LANES // 2, axis=1), y).astype(BF16)

    if sides == 2:
        @pl.when(rng == 0)
        def _():
            packs_in[0, :, 0] = jnp.zeros((groups, height, LANES), BF16)

        @pl.when(rng == rng_axis - 1)
        def _():
            packs_in[0, :, 1] = jnp.zeros((groups, height, LANES), BF16)

    peers = 1
    for cond in (has_prev, has_left, has_right):
        peers = peers + cond.astype(jnp.int32)
    pl.semaphore_wait(barrier, peers)

    def send(pieces):
        @pl.when(has_prev)
        def _():
            for piece in pieces:
                for copy in z_copies(piece, date - 1):
                    copy.start()

    send([word[1:] for word in FIRST])
    for copy in own_rows:
        copy.start()
    for copy in own:
        copy.wait()
    for g in range(groups):
        pack(g, 0)

    @pl.when(date == dates_axis - 1)
    def _():
        tiles[dates:] = jnp.zeros((dates, PARTS, BLOCKS, height, LANES), BF16)
        packs_in[1] = jnp.zeros((groups, sides, height, LANES), BF16)

    frame = (1 - rng, rng) if sides == 1 else tuple(range(BLOCKS))

    def column_of(index):
        return jnp.where(index < LANES, LANES * frame[0], LANES * (frame[1] - 1)) + index

    col_out = column_of(lax.broadcasted_iota(jnp.int32, (cols, cols), 1))
    col_in = column_of(lax.broadcasted_iota(jnp.int32, (cols, cols), 0))
    band[...] = (jnp.abs(col_in - col_out) <= HALF_RG).astype(F32).astype(BF16)
    edge_in = lax.broadcasted_iota(jnp.int32, (LANES, LANES), 0)
    edge_out = lax.broadcasted_iota(jnp.int32, (LANES, LANES), 1)
    for side in range(sides):
        left = left_of(side)
        gap = (edge_in & (EDGE - 1)) - (edge_out & (EDGE - 1)) + EDGE - 2 * EDGE * left
        near = (slot_of(edge_in, left) == slot_of(edge_out, 1 - left)) & (jnp.abs(gap) <= HALF_RG)
        diag[side] = near.astype(F32).astype(BF16)

    line_out = lax.broadcasted_iota(jnp.int32, (lines, height), 0)
    row = lax.broadcasted_iota(jnp.int32, (lines, height), 1)
    line_in = row - jnp.where(row >= lines, az * height, 0)
    pick[...] = (jnp.abs(line_in - line_out) <= HALF_AZ).astype(F32).astype(BF16)

    def line_sums(rows):
        return jnp.dot(pick[...], rows, preferred_element_type=F32)

    def column_sums(rows):
        return jnp.dot(jnp.concatenate(rows, axis=0), band[...], preferred_element_type=F32)

    def halves(x):
        hi = x.astype(BF16)
        return hi, (x - hi.astype(F32)).astype(BF16)

    def part(e, i):
        return jnp.concatenate([tiles[e, i, b] for b in frame], axis=1)

    def twice():
        return jnp.concatenate([pick[...]] * 2, axis=1)

    lane = lax.broadcasted_iota(jnp.int32, (lines, LANES), 1)

    def with_edges(x, read, slot):
        out = [x[:, b * LANES:(b + 1) * LANES] for b in range(BLOCKS)]
        for side in range(sides):
            y = read(side)
            y = pltpu.roll(y, LANES - EDGE * slot, axis=1) if slot else y
            mine = slot_of(lane, 1 - left_of(side)) == 0
            out[side * (BLOCKS - 1)] += jnp.where(mine, y, 0.0)
        return jnp.concatenate(out, axis=1)

    def put(ref, value):
        for b in range(BLOCKS):
            if sides == 1:
                ref[:, pl.ds(pl.multiple_of(frame[b] * LANES, LANES), LANES)] = value[:, b * LANES:(b + 1) * LANES]
            else:
                ref[:, b * LANES:(b + 1) * LANES] = value[:, b * LANES:(b + 1) * LANES]

    def edges_of(late):
        early, tasks = [], []

        def power_task(side):
            box = []

            def first():
                a0 = edges[late, side, 0].astype(F32)
                a1 = edges[late, side, 1].astype(F32)
                z = jnp.dot(twice(), jnp.concatenate(halves(a0 * a0 + a1 * a1), axis=0), preferred_element_type=F32)
                box.extend(halves(z))

            def second():
                y = jnp.dot(jnp.concatenate(box, axis=0), diag[side], preferred_element_type=F32)
                edge_power[late, side] = y[0:lines] + y[lines:]

            return first, second

        def cross_task(side, group):
            box = []

            def first():
                a0, a1 = edges[0, side, 0], edges[0, side, 1]
                for lag in group:
                    b = [edges[late, side, i] for i in range(PARTS)]
                    if lag < LAG_MAX:
                        b = [pltpu.roll(x.astype(F32), LANES - EDGE * lag, axis=1).astype(BF16) for x in b]
                    z = line_sums(jnp.concatenate([a0 * b[0] + a1 * b[1], a1 * b[0] - a0 * b[1]], axis=1)).astype(BF16)
                    box.extend([z[:, 0:LANES], z[:, LANES:]])

            def second():
                y = jnp.dot(jnp.concatenate(box, axis=0), diag[side], preferred_element_type=F32)
                for i, lag in enumerate(group):
                    for part in range(PARTS):
                        at = (2 * i + part) * lines
                        edge_cross[late, side, lag - 1, part] = y[at:at + lines]

            return first, second

        for side in range(sides):
            early.append(power_task(side))
            lags_here = list(range(1, LAG_MAX + late))
            for start in range(0, len(lags_here), 4):
                tasks.append(cross_task(side, lags_here[start:start + 4]))
        return {"P": early, "Q": tasks}

    def powers_of(e):
        box = []

        def first():
            a0 = part(e, 0).astype(F32)
            a1 = part(e, 1).astype(F32)
            p = a0 * a0 + a1 * a1
            z = jnp.dot(twice(), jnp.concatenate(halves(p), axis=0), preferred_element_type=F32)
            box.extend(halves(z))
            box.append(p[0:lines] if e < dates else None)

        def second():
            y = column_sums(box[0:2])
            y = with_edges(y[0:lines] + y[lines:], lambda side: edge_power[e // dates, side], e % dates)
            m = y * (1.0 / LOOKS) + EPS
            r = 1.0 / m
            put(logs.at[e], jnp.log(m))
            inv[e] = r * (1.0 / LOOKS)
            if e < dates:
                put(mean.at[e], m)
                term = box[2] * r
                if e == 0:
                    acc[...] = term
                else:
                    acc[...] += term

        return [(first, second)]

    def pairs_of(e):
        tasks = []
        first, last = (0, e) if e < dates else (e - dates, dates)
        for start in range(first, last, BATCH):
            tasks.append(pair_task(e, range(start, min(start + BATCH, last))))
        return tasks

    def pair_task(e, group):
        box = []

        def first():
            b0, b1 = part(e, 0), part(e, 1)
            for d in group:
                a0, a1 = part(d, 0), part(d, 1)
                z = line_sums(jnp.concatenate([a0 * b0 + a1 * b1, a1 * b0 - a0 * b1], axis=1)).astype(BF16)
                box.extend([z[:, 0:cols], z[:, cols:]])

        def second():
            y = column_sums(box)
            for i, d in enumerate(group):
                sr = y[2 * i * lines:(2 * i + 1) * lines]
                si = y[(2 * i + 1) * lines:(2 * i + 2) * lines]
                lag = e - d
                sr = with_edges(sr, lambda side: edge_cross[e // dates, side, lag - 1, 0], d)
                si = with_edges(si, lambda side: edge_cross[e // dates, side, lag - 1, 1], d)
                put(coh.at[e, lag - 1], ((sr * sr + si * si) * (inv[d] * inv[e])).astype(BF16))

        return first, second

    def run_tasks(tasks):
        late = []
        for first, second in tasks:
            first()
            late.append(second)
            if len(late) > DEPTH:
                late.pop(0)()
        for second in late:
            second()

    def chain(way, to):
        return pltpu.make_async_remote_copy(
            src_ref=chain_out.at[way], dst_ref=chain_in.at[way],
            send_sem=c_send.at[way], recv_sem=c_recv.at[way],
            device_id={"date": to}, device_id_type=pl.DeviceIdType.MESH)

    def up_step(first):
        if not first:
            chain(0, date + 1).wait_recv()

        @pl.when(has_next)
        def _():
            s = acc[...] if first else acc[...] + chain_in[0].astype(F32)
            chain_out[0] = s.astype(BF16)
            chain(0, date + 1).start()

    def down_step(first):
        if not first:
            chain(1, date - 1).wait_recv()

        @pl.when(has_prev)
        def _():
            s = acc[...] if first else acc[...] + chain_in[1].astype(F32)
            chain_out[1] = s.astype(BF16)
            chain(1, date - 1).start()

    def chain_point(k, last):
        if last:
            pl.when(date >= k)(lambda: up_step(False))
            pl.when(date <= dates_axis - 1 - k)(lambda: down_step(False))
        else:
            pl.when(date == dates_axis - 1 - k)(lambda: down_step(k == 0))
            pl.when(date == k)(lambda: up_step(k == 0))

    def filtered():
        lag_copy.wait()
        up = jnp.where(has_prev, chain_in[0].astype(F32), 0.0)
        down = jnp.where(has_next, chain_in[1].astype(F32), 0.0)
        put(total, (acc[...] + up + down) * (1.0 / float(dates * dates_axis)))

    @pl.when(date == 0)
    def _():
        chain_in[0] = jnp.zeros((lines, cols), BF16)

    @pl.when(date == dates_axis - 1)
    def _():
        chain_in[1] = jnp.zeros((lines, cols), BF16)

    def z_wait(piece):
        for copy in z_copies(piece, date - 1):
            copy.wait_recv()

    def next_step(kind, i):
        if kind == "U":
            z_wait("p0")
        elif kind == "B":
            z_wait("b%d" % i)
            for copy in a_copies(i):
                copy.start()
        elif kind == "V":
            for copy in a_copies(i):
                copy.wait_recv()
        elif kind == "F":
            z_wait("f%d" % i)

    for copy in own_rows:
        copy.wait_recv()
    for g in range(groups):
        pack(g, 1)
    more = {}
    points = sum(word[0] == "K" for word in ORDER)
    todo = [(word[0], word[1:]) for word in ORDER]
    while todo:
        kind, i = todo.pop(0)
        if kind == "S":
            run = [i]
            while todo and todo[0][0] == "S":
                run.append(todo.pop(0)[1])
            send(run)
        elif kind == "T":
            filtered()
        elif kind == "X":
            for g in range(groups):
                x_wait(g)
            unpack(0)
            more = edges_of(0)
        elif kind in "PQ":
            tasks = more.pop(kind, []) + (powers_of if kind == "P" else pairs_of)(int(i))
            while todo and todo[0][0] in "PQ":
                kind, i = todo.pop(0)
                tasks += more.pop(kind, []) + (powers_of if kind == "P" else pairs_of)(int(i))
            run_tasks(tasks)
        elif kind == "K":
            if int(i) < dates_axis:
                chain_point(int(i), int(i) == points - 1)
        else:
            run = [(kind, int(i))]
            while todo and todo[0][0] in "BUVF":
                run.append((todo[0][0], int(todo.pop(0)[1])))

            @pl.when(has_next)
            def _():
                for step in run:
                    next_step(*step)
            if "U" in [step[0] for step in run]:
                unpack(1)
                more = edges_of(1)

    for copy in own_rows:
        copy.wait_send()
    for g in range(groups):
        for tail in range(2):
            x_each(g, tail, lambda c: c.wait_send())

    @pl.when(has_next)
    def _():
        for g in range(groups):
            for copy in a_copies(g):
                copy.wait_send()
        chain(0, date + 1).wait_send()

    @pl.when(has_prev)
    def _():
        for word in FIRST + [w for w in ORDER if w[0] == "S"]:
            for copy in z_copies(word[1:], date - 1):
                copy.wait_send()
        chain(1, date - 1).wait_send()


def pick_kernel(sizes, lags_in, coh, logs, mean, total, coh_out, log_out, queg_out,
                lags, zero, ratio, queg, lag_sem, coh_sem, log_sem, queg_sem):
    dates, slots, lines, cols = sizes
    lag_copy = pltpu.make_async_copy(lags_in, lags, lag_sem)
    lag_copy.start()
    for d in range(dates):
        queg[d] = mean[d] * total[...]
    queg_copy = pltpu.make_async_copy(queg, queg_out, queg_sem)
    queg_copy.start()
    zero[...] = jnp.zeros((lines, cols), BF16)
    lag_copy.wait()

    def start(d, carry):
        for s in range(slots):
            lag = lags[d, s]

            @pl.when(lag > 0)
            def _():
                pltpu.make_async_copy(coh.at[d + lag, lag - 1], coh_out.at[d, s], coh_sem).start()

            @pl.when(lag <= 0)
            def _():
                pltpu.make_async_copy(zero, coh_out.at[d, s], coh_sem).start()
        return carry

    lax.fori_loop(0, dates, start, 0)

    def each(d, carry):
        for s in range(slots):
            lag = lags[d, s]
            there = d + jnp.maximum(lag, 0)
            keep = jnp.broadcast_to(lag > 0, (lines, cols))
            ratio[d, s] = jnp.where(keep, logs[d] - logs[there], 0.0).astype(BF16)
        pltpu.make_async_copy(ratio.at[d], log_out.at[d], log_sem).start()
        return carry

    lax.fori_loop(0, dates, each, 0)
    pltpu.make_async_copy(ratio, coh_out, coh_sem).wait()
    pltpu.make_async_copy(ratio, log_out, log_sem).wait()
    queg_copy.wait()


def solution(mesh):
    dates_axis, rng_axis, az_axis = mesh.shape["date"], mesh.shape["rng"], mesh.shape["az"]
    assert az_axis == 2 and rng_axis > 1
    sides = 1 if rng_axis == 2 else 2

    def on_device(slc, lags):
        dates, parts, lines, cols = slc.shape
        slots = lags.shape[1]
        assert cols == BLOCKS * LANES and dates == LAG_MAX and parts == PARTS and dates == 2 * GROUP
        groups = dates // GROUP
        pieces = 1 + dates + groups
        held = 4 * lines * cols * (LAG_MAX * dates + 3 * dates + 1) + 4 * 8 * LANES
        height = lines + ROWS
        inside = pl.BlockSpec(memory_space=pltpu.VMEM)
        anywhere = pl.BlockSpec(memory_space=pltpu.HBM)
        field = (lines, cols)
        dma = pltpu.SemaphoreType.DMA
        coh, logs, mean, total, lags = pl.pallas_call(
            functools.partial(gather_kernel, (dates_axis, rng_axis, dates, lines, cols)),
            out_shape=[
                jax.ShapeDtypeStruct((2 * dates, LAG_MAX, *field), BF16),
                jax.ShapeDtypeStruct((2 * dates, *field), F32),
                jax.ShapeDtypeStruct((dates, *field), F32),
                jax.ShapeDtypeStruct(field, F32),
                jax.ShapeDtypeStruct(lags.shape, lags.dtype),
            ],
            in_specs=[anywhere] * 2,
            out_specs=[inside] * 5,
            scratch_shapes=[
                pltpu.VMEM((2 * dates, parts, BLOCKS, height, LANES), BF16),
                pltpu.VMEM((groups, sides, height, LANES), BF16),
                pltpu.VMEM((2, groups, sides, height, LANES), BF16),
                pltpu.VMEM((2, sides, parts, height, LANES), BF16),
                pltpu.VMEM((2, sides, lines, LANES), F32),
                pltpu.VMEM((2, sides, LAG_MAX, parts, lines, LANES), F32),
                pltpu.VMEM((cols, cols), BF16),
                pltpu.VMEM((sides, LANES, LANES), BF16),
                pltpu.VMEM((lines, height), BF16),
                pltpu.VMEM((2 * dates, *field), F32),
                pltpu.VMEM(field, F32),
                pltpu.VMEM((2, *field), BF16),
                pltpu.VMEM((2, *field), BF16),
                dma((BLOCKS,)), dma, dma((pieces, BLOCKS)), dma((pieces, BLOCKS)),
                dma((1 + groups, BLOCKS)), dma((1 + groups, BLOCKS)),
                dma((sides, groups, 2)), dma((sides, groups, 2)),
                dma((2,)), dma((2,)),
            ],
            compiler_params=pltpu.CompilerParams(collective_id=0, has_side_effects=True, vmem_limit_bytes=VMEM_BYTES - SPARE - held),
            name="gather",
        )(pltpu.with_memory_space_constraint(slc, pltpu.HBM), pltpu.with_memory_space_constraint(lags, pltpu.HBM))
        return pl.pallas_call(
            functools.partial(pick_kernel, (dates, slots, lines, cols)),
            out_shape=[
                jax.ShapeDtypeStruct((dates, slots, *field), BF16),
                jax.ShapeDtypeStruct((dates, slots, *field), BF16),
                jax.ShapeDtypeStruct((dates, *field), F32),
            ],
            in_specs=[inside] * 5,
            out_specs=[anywhere] * 3,
            scratch_shapes=[
                pltpu.SMEM((dates, slots), jnp.int32),
                pltpu.VMEM(field, BF16),
                pltpu.VMEM((dates, slots, *field), BF16),
                pltpu.VMEM((dates, *field), F32),
                dma, dma, dma, dma,
            ],
            compiler_params=pltpu.CompilerParams(vmem_limit_bytes=16 * 2 ** 20),
            name="pick",
        )(lags, coh, logs, mean, total)

    return jax.shard_map(
        on_device,
        mesh=mesh,
        in_specs=(P(("slab", "date"), None, "az", "rng"), P("date", None)),
        out_specs=(
            P(("slab", "date"), None, "az", "rng"),
            P(("slab", "date"), None, "az", "rng"),
            P(("slab", "date"), "az", "rng"),
        ),
        check_vma=False,
    )
```

```python
import functools

import jax
import jax.numpy as jnp
from jax import lax
from jax.experimental import pallas as pl
from jax.experimental.pallas import tpu as pltpu
from jax.sharding import PartitionSpec as P

HALF_AZ = 2
HALF_RG = 10
LAG_MAX = 8
EPS = 1e-05
LOOKS = float((2 * HALF_AZ + 1) * (2 * HALF_RG + 1))

LANES = 128
ROWS = 16
EDGE = 16
PARTS = 2
BLOCKS = 2
LP = True
DEPTH = 1
GROUP = LANES // (EDGE * PARTS)
BATCH = 4
VMEM_BYTES = 67043328
SPARE = 16 * 2 ** 20
F32 = jnp.float32
BF16 = jnp.bfloat16

ORDER = [
    "X0 Sp0 P0 P1",
    "P2 P3 P4 P5",
    "P6 P7 B0 K0",
    "Sf2 Sf3 Sb1 Q1",
    "Q2 Q3 Q4 Q5",
    "Q6 Q7 V0 U0",
    "F0 P8 K1 Sf4",
    "Sf5 Sf6 Sf7 Q8",
    "F1 P9 Q9 F2",
    "P10 Q10 K2 F3",
    "P11 Q11 B1 V1",
    "F4 P12 Q12 F5",
    "P13 Q13 F6 P14",
    "Q14 F7 P15 Q15",
    "K3 T",
]
ORDER = [word for words in ORDER for word in words.split()]
FIRST = ["Sb0", "Sf0", "Sf1"]


def gather_kernel(sizes, slc, lags_in, coh, logs, mean, total, lags,
                  tiles, packs_out, packs_in, edges, edge_power, edge_cross, band, diag, pick, inv, acc, chain_out, chain_in,
                  own_sem, lag_sem, z_send, z_recv, a_send, a_recv, x_send, x_recv,
                  c_send, c_recv):
    dates_axis, rng_axis, dates, lines, cols = sizes
    sides = 1 if rng_axis == 2 else 2
    groups = dates // GROUP
    date = lax.axis_index("date")
    rng = lax.axis_index("rng")
    az = lax.axis_index("az")
    has_next = date < dates_axis - 1
    has_prev = date > 0
    has_right = rng < rng_axis - 1
    has_left = rng > 0
    peer = 1 - az
    height = lines + ROWS

    barrier = pltpu.get_barrier_semaphore()

    def greet(where):
        pl.semaphore_signal(barrier, inc=1, device_id=where, device_id_type=pl.DeviceIdType.MESH)

    greet({"az": peer})
    pl.when(has_next)(lambda: greet({"date": date + 1}))
    pl.when(has_left)(lambda: greet({"rng": rng - 1}))
    pl.when(has_right)(lambda: greet({"rng": rng + 1}))

    def block_of(b):
        return pl.ds(b * LANES if isinstance(b, int) else pl.multiple_of(b * LANES, LANES), LANES)

    own = [
        pltpu.make_async_copy(
            slc.at[:, :, :, block_of(b)], tiles.at[pl.ds(0, dates), :, b, pl.ds(0, lines), :], own_sem.at[b])
        for b in range(BLOCKS)]
    for copy in own:
        copy.start()
    lag_copy = pltpu.make_async_copy(lags_in, lags, lag_sem)
    lag_copy.start()

    border = pl.multiple_of((1 - az) * (lines - ROWS), ROWS)
    rest = pl.multiple_of(az * ROWS, ROWS)

    def z_copies(piece, to):
        kind, i = piece[0], int(piece[1:])
        if kind == "p":
            return [pltpu.make_async_remote_copy(
                src_ref=packs_in.at[0], dst_ref=packs_in.at[1],
                send_sem=z_send.at[0, 0], recv_sem=z_recv.at[0, 0],
                device_id={"date": to}, device_id_type=pl.DeviceIdType.MESH)]
        if kind == "b":
            first, count, row, rows, k = i * GROUP, GROUP, border, ROWS, 1 + i
        else:
            first, count, row, rows, k = i, 1, rest, lines - ROWS, 1 + groups + i
        return [
            pltpu.make_async_remote_copy(
                src_ref=slc.at[pl.ds(first, count), :, pl.ds(row, rows), block_of(b)],
                dst_ref=tiles.at[pl.ds(dates + first, count), :, b, pl.ds(row, rows), :],
                send_sem=z_send.at[k, b], recv_sem=z_recv.at[k, b],
                device_id={"date": to}, device_id_type=pl.DeviceIdType.MESH)
            for b in range(BLOCKS)]

    own_rows = [
        pltpu.make_async_remote_copy(
            src_ref=slc.at[:, :, pl.ds(border, ROWS), block_of(b)],
            dst_ref=tiles.at[pl.ds(0, dates), :, b, pl.ds(lines, ROWS), :],
            send_sem=a_send.at[0, b], recv_sem=a_recv.at[0, b],
            device_id={"az": peer}, device_id_type=pl.DeviceIdType.MESH)
        for b in range(BLOCKS)]

    def a_copies(g):
        where = pl.ds(dates + g * GROUP, GROUP)
        return [
            pltpu.make_async_remote_copy(
                src_ref=tiles.at[where, :, b, pl.ds(border, ROWS), :],
                dst_ref=tiles.at[where, :, b, pl.ds(lines, ROWS), :],
                send_sem=a_send.at[1 + g, b], recv_sem=a_recv.at[1 + g, b],
                device_id={"az": peer}, device_id_type=pl.DeviceIdType.MESH)
            for b in range(BLOCKS)]

    def x_copy(g, tail, side, to):
        rows = pl.ds(lines, ROWS) if tail else pl.ds(0, lines)
        return pltpu.make_async_remote_copy(
            src_ref=packs_out.at[g, side, rows, :],
            dst_ref=packs_in.at[0, g, side, rows, :],
            send_sem=x_send.at[side, g, tail], recv_sem=x_recv.at[side, g, tail],
            device_id={"rng": to}, device_id_type=pl.DeviceIdType.MESH)

    def x_each(g, tail, act):
        if sides == 1:
            act(x_copy(g, tail, 0, 1 - rng))
        else:
            pl.when(has_right)(lambda: act(x_copy(g, tail, 0, rng + 1)))
            pl.when(has_left)(lambda: act(x_copy(g, tail, 1, rng - 1)))

    def x_wait(g):
        for tail in range(2):
            if sides == 1:
                x_copy(g, tail, 0, 1 - rng).wait_recv()
            else:
                pl.when(has_left)(lambda: x_copy(g, tail, 0, rng - 1).wait_recv())
                pl.when(has_right)(lambda: x_copy(g, tail, 1, rng + 1).wait_recv())

    def left_of(side):
        return rng if sides == 1 else 1 - side

    def slot_of(lane, left):
        return lax.shift_right_logical((lane + EDGE * left) & (LANES - 1), EDGE.bit_length() - 1)

    def pack(g, tail):
        first, rows = (lines, ROWS) if tail else (0, lines)
        lane = lax.broadcasted_iota(jnp.int32, (rows, LANES), 1)
        for side in range(sides):
            high = 1 - rng if sides == 1 else 1 - side
            block = 1 - rng if sides == 1 else (1 - side) * (BLOCKS - 1)
            slot = slot_of(lane, high)
            out = None
            for s in range(GROUP * PARTS):
                x = tiles[g * GROUP + s % GROUP, s // GROUP, block, first:first + rows, :].astype(F32)
                out = x if s == 0 else jnp.where(slot == s, pltpu.roll(x, EDGE * s, axis=1), out)
            packs_out[g, side, first:first + rows] = out.astype(BF16)
        x_each(g, tail, lambda c: c.start())

    def unpack(late):
        lane = lax.broadcasted_iota(jnp.int32, (height, LANES), 1)
        for side in range(sides):
            lower = slot_of(lane, left_of(side)) < GROUP
            x = packs_in[late, 0, side].astype(F32)
            y = packs_in[late, 1, side].astype(F32)
            edges[late, side, 0] = jnp.where(lower, x, pltpu.roll(y, LANES // 2, axis=1)).astype(BF16)
            edges[late, side, 1] = jnp.where(lower, pltpu.roll(x, LANES // 2, axis=1), y).astype(BF16)

    if sides == 2:
        @pl.when(rng == 0)
        def _():
            packs_in[0, :, 0] = jnp.zeros((groups, height, LANES), BF16)

        @pl.when(rng == rng_axis - 1)
        def _():
            packs_in[0, :, 1] = jnp.zeros((groups, height, LANES), BF16)

    peers = 1
    for cond in (has_prev, has_left, has_right):
        peers = peers + cond.astype(jnp.int32)
    pl.semaphore_wait(barrier, peers)

    def send(pieces):
        @pl.when(has_prev)
        def _():
            for piece in pieces:
                for copy in z_copies(piece, date - 1):
                    copy.start()

    send([word[1:] for word in FIRST])
    for copy in own_rows:
        copy.start()
    for copy in own:
        copy.wait()
    for g in range(groups):
        pack(g, 0)

    coh[0, 0] = jnp.zeros((lines, cols), BF16)

    @pl.when(date == dates_axis - 1)
    def _():
        tiles[dates:] = jnp.zeros((dates, PARTS, BLOCKS, height, LANES), BF16)
        packs_in[1] = jnp.zeros((groups, sides, height, LANES), BF16)

    frame = (1 - rng, rng) if sides == 1 else tuple(range(BLOCKS))

    def column_of(index):
        return jnp.where(index < LANES, LANES * frame[0], LANES * (frame[1] - 1)) + index

    col_out = column_of(lax.broadcasted_iota(jnp.int32, (cols, cols), 1))
    col_in = column_of(lax.broadcasted_iota(jnp.int32, (cols, cols), 0))
    band[...] = (jnp.abs(col_in - col_out) <= HALF_RG).astype(F32).astype(BF16)
    edge_in = lax.broadcasted_iota(jnp.int32, (LANES, LANES), 0)
    edge_out = lax.broadcasted_iota(jnp.int32, (LANES, LANES), 1)
    for side in range(sides):
        left = left_of(side)
        gap = (edge_in & (EDGE - 1)) - (edge_out & (EDGE - 1)) + EDGE - 2 * EDGE * left
        near = (slot_of(edge_in, left) == slot_of(edge_out, 1 - left)) & (jnp.abs(gap) <= HALF_RG)
        diag[side] = near.astype(F32).astype(BF16)

    line_out = lax.broadcasted_iota(jnp.int32, (lines, height), 0)
    row = lax.broadcasted_iota(jnp.int32, (lines, height), 1)
    line_in = row - jnp.where(row >= lines, az * height, 0)
    pick[...] = (jnp.abs(line_in - line_out) <= HALF_AZ).astype(F32).astype(BF16)

    def line_sums(rows):
        return jnp.dot(pick[...], rows, preferred_element_type=F32)

    def column_sums(rows):
        return jnp.dot(jnp.concatenate(rows, axis=0), band[...], preferred_element_type=F32)

    def halves(x):
        hi = x.astype(BF16)
        return hi, (x - hi.astype(F32)).astype(BF16)

    def part(e, i):
        return jnp.concatenate([tiles[e, i, b] for b in frame], axis=1)

    def twice():
        return jnp.concatenate([pick[...]] * 2, axis=1)

    lane = lax.broadcasted_iota(jnp.int32, (lines, LANES), 1)

    def with_edges(x, read, slot):
        out = [x[:, b * LANES:(b + 1) * LANES] for b in range(BLOCKS)]
        for side in range(sides):
            y = read(side)
            y = pltpu.roll(y, LANES - EDGE * slot, axis=1) if slot else y
            mine = slot_of(lane, 1 - left_of(side)) == 0
            out[side * (BLOCKS - 1)] += jnp.where(mine, y, 0.0)
        return jnp.concatenate(out, axis=1)

    def put(ref, value):
        for b in range(BLOCKS):
            if sides == 1:
                ref[:, pl.ds(pl.multiple_of(frame[b] * LANES, LANES), LANES)] = value[:, b * LANES:(b + 1) * LANES]
            else:
                ref[:, b * LANES:(b + 1) * LANES] = value[:, b * LANES:(b + 1) * LANES]

    def edges_of(late):
        early, tasks = [], []

        def power_task(side):
            box = []

            def first():
                a0 = edges[late, side, 0].astype(F32)
                a1 = edges[late, side, 1].astype(F32)
                z = jnp.dot(twice(), jnp.concatenate(halves(a0 * a0 + a1 * a1), axis=0), preferred_element_type=F32)
                box.extend(halves(z))

            def second():
                y = jnp.dot(jnp.concatenate(box, axis=0), diag[side], preferred_element_type=F32)
                edge_power[late, side] = y[0:lines] + y[lines:]

            return first, second

        def cross_task(side, group):
            box = []

            def first():
                a0, a1 = edges[0, side, 0], edges[0, side, 1]
                for lag in group:
                    b = [edges[late, side, i] for i in range(PARTS)]
                    if lag < LAG_MAX:
                        b = [pltpu.roll(x.astype(F32), LANES - EDGE * lag, axis=1).astype(BF16) for x in b]
                    z = line_sums(jnp.concatenate([a0 * b[0] + a1 * b[1], a1 * b[0] - a0 * b[1]], axis=1)).astype(BF16)
                    box.extend([z[:, 0:LANES], z[:, LANES:]])

            def second():
                y = jnp.dot(jnp.concatenate(box, axis=0), diag[side], preferred_element_type=F32)
                for i, lag in enumerate(group):
                    for part in range(PARTS):
                        at = (2 * i + part) * lines
                        edge_cross[late, side, lag - 1, part] = y[at:at + lines]

            return first, second

        for side in range(sides):
            early.append(power_task(side))
            lags_here = list(range(1, LAG_MAX + late))
            for start in range(0, len(lags_here), 4):
                tasks.append(cross_task(side, lags_here[start:start + 4]))
        return {"P": early, "Q": tasks}

    def powers_of(e):
        box = []

        def first():
            a0 = part(e, 0).astype(F32)
            a1 = part(e, 1).astype(F32)
            p = a0 * a0 + a1 * a1
            z = jnp.dot(twice(), jnp.concatenate(halves(p), axis=0), preferred_element_type=F32)
            box.extend(halves(z))
            box.append(p[0:lines] if e < dates else None)

        def second():
            y = column_sums(box[0:2])
            y = with_edges(y[0:lines] + y[lines:], lambda side: edge_power[e // dates, side], e % dates)
            m = y * (1.0 / LOOKS) + EPS
            r = 1.0 / m
            put(logs.at[e], jnp.log(m))
            inv[e] = r * (1.0 / LOOKS)
            if e < dates:
                put(mean.at[e], m)
                term = box[2] * r
                if e == 0:
                    acc[...] = term
                else:
                    acc[...] += term

        return [(first, second)]

    def pairs_of(e):
        tasks = []
        first, last = (0, e) if e < dates else (e - dates, dates)
        for start in range(first, last, BATCH):
            tasks.append(pair_task(e, range(start, min(start + BATCH, last))))
        return tasks

    def pair_task(e, group):
        box = []

        def first():
            b0, b1 = part(e, 0), part(e, 1)
            for d in group:
                a0, a1 = part(d, 0), part(d, 1)
                z = line_sums(jnp.concatenate([a0 * b0 + a1 * b1, a1 * b0 - a0 * b1], axis=1)).astype(BF16)
                box.extend([z[:, 0:cols], z[:, cols:]])

        def second():
            y = column_sums(box)
            for i, d in enumerate(group):
                sr = y[2 * i * lines:(2 * i + 1) * lines]
                si = y[(2 * i + 1) * lines:(2 * i + 2) * lines]
                lag = e - d
                sr = with_edges(sr, lambda side: edge_cross[e // dates, side, lag - 1, 0], d)
                si = with_edges(si, lambda side: edge_cross[e // dates, side, lag - 1, 1], d)
                put(coh.at[e, lag - 1], ((sr * sr + si * si) * (inv[d] * inv[e])).astype(BF16))

        return first, second

    def run_tasks(tasks):
        late = []
        for first, second in tasks:
            first()
            late.append(second)
            if len(late) > DEPTH:
                late.pop(0)()
        for second in late:
            second()

    def chain(way, to):
        return pltpu.make_async_remote_copy(
            src_ref=chain_out.at[way], dst_ref=chain_in.at[way],
            send_sem=c_send.at[way], recv_sem=c_recv.at[way],
            device_id={"date": to}, device_id_type=pl.DeviceIdType.MESH)

    def up_step(first):
        if not first:
            chain(0, date + 1).wait_recv()

        @pl.when(has_next)
        def _():
            s = acc[...] if first else acc[...] + chain_in[0].astype(F32)
            chain_out[0] = s.astype(BF16)
            chain(0, date + 1).start()

    def down_step(first):
        if not first:
            chain(1, date - 1).wait_recv()

        @pl.when(has_prev)
        def _():
            s = acc[...] if first else acc[...] + chain_in[1].astype(F32)
            chain_out[1] = s.astype(BF16)
            chain(1, date - 1).start()

    def chain_point(k, last):
        if last:
            pl.when(date >= k)(lambda: up_step(False))
            pl.when(date <= dates_axis - 1 - k)(lambda: down_step(False))
        else:
            pl.when(date == dates_axis - 1 - k)(lambda: down_step(k == 0))
            pl.when(date == k)(lambda: up_step(k == 0))

    def filtered():
        lag_copy.wait()
        up = jnp.where(has_prev, chain_in[0].astype(F32), 0.0)
        down = jnp.where(has_next, chain_in[1].astype(F32), 0.0)
        put(total, (acc[...] + up + down) * (1.0 / float(dates * dates_axis)))

    @pl.when(date == 0)
    def _():
        chain_in[0] = jnp.zeros((lines, cols), BF16)

    @pl.when(date == dates_axis - 1)
    def _():
        chain_in[1] = jnp.zeros((lines, cols), BF16)

    def z_wait(piece):
        for copy in z_copies(piece, date - 1):
            copy.wait_recv()

    def next_step(kind, i):
        if kind == "U":
            z_wait("p0")
        elif kind == "B":
            z_wait("b%d" % i)
            for copy in a_copies(i):
                copy.start()
        elif kind == "V":
            for copy in a_copies(i):
                copy.wait_recv()
        elif kind == "F":
            z_wait("f%d" % i)

    for copy in own_rows:
        copy.wait_recv()
    for g in range(groups):
        pack(g, 1)
    more = {}
    points = sum(word[0] == "K" for word in ORDER)
    todo = [(word[0], word[1:]) for word in ORDER]
    while todo:
        kind, i = todo.pop(0)
        if kind == "S":
            run = [i]
            while todo and todo[0][0] == "S":
                run.append(todo.pop(0)[1])
            send(run)
        elif kind == "T":
            filtered()
        elif kind == "X":
            for g in range(groups):
                x_wait(g)
            unpack(0)
            more = edges_of(0)
        elif kind in "PQ":
            tasks = more.pop(kind, []) + (powers_of if kind == "P" else pairs_of)(int(i))
            while todo and todo[0][0] in "PQ":
                kind, i = todo.pop(0)
                tasks += more.pop(kind, []) + (powers_of if kind == "P" else pairs_of)(int(i))
            run_tasks(tasks)
        elif kind == "K":
            if int(i) < dates_axis:
                chain_point(int(i), int(i) == points - 1)
        else:
            run = [(kind, int(i))]
            while todo and todo[0][0] in "BUVF":
                run.append((todo[0][0], int(todo.pop(0)[1])))

            @pl.when(has_next)
            def _():
                for step in run:
                    next_step(*step)
            if "U" in [step[0] for step in run]:
                unpack(1)
                more = edges_of(1)

    for copy in own_rows:
        copy.wait_send()
    for g in range(groups):
        for tail in range(2):
            x_each(g, tail, lambda c: c.wait_send())

    @pl.when(has_next)
    def _():
        for g in range(groups):
            for copy in a_copies(g):
                copy.wait_send()
        chain(0, date + 1).wait_send()

    @pl.when(has_prev)
    def _():
        for word in FIRST + [w for w in ORDER if w[0] == "S"]:
            for copy in z_copies(word[1:], date - 1):
                copy.wait_send()
        chain(1, date - 1).wait_send()


def pick_kernel(sizes, lags_in, coh, logs, mean, total, coh_out, log_out, queg_out,
                lags, ratio, queg, lag_sem, coh_sem, log_sem, queg_sem):
    dates, slots, lines, cols = sizes
    lag_copy = pltpu.make_async_copy(lags_in, lags, lag_sem)
    lag_copy.start()
    for d in range(dates):
        queg[d] = mean[d] * total[...]
    queg_copy = pltpu.make_async_copy(queg, queg_out, queg_sem)
    queg_copy.start()
    lag_copy.wait()

    def each(d, carry):
        for s in range(slots):
            lag = lags[d, s]
            there = d + jnp.maximum(lag, 0)
            pltpu.make_async_copy(
                coh.at[jnp.where(lag > 0, there, 0), jnp.maximum(lag, 1) - 1], coh_out.at[d, s], coh_sem).start()
            keep = jnp.broadcast_to(lag > 0, (lines, cols))
            ratio[d, s] = jnp.where(keep, logs[d] - logs[there], 0.0).astype(BF16)
        pltpu.make_async_copy(ratio.at[d], log_out.at[d], log_sem).start()
        return carry

    lax.fori_loop(0, dates, each, 0, unroll=1)
    pltpu.make_async_copy(ratio, coh_out, coh_sem).wait()
    pltpu.make_async_copy(ratio, log_out, log_sem).wait()
    queg_copy.wait()


def solution(mesh):
    dates_axis, rng_axis, az_axis = mesh.shape["date"], mesh.shape["rng"], mesh.shape["az"]
    assert az_axis == 2 and rng_axis > 1
    sides = 1 if rng_axis == 2 else 2

    def on_device(slc, lags):
        dates, parts, lines, cols = slc.shape
        slots = lags.shape[1]
        assert cols == BLOCKS * LANES and dates == LAG_MAX and parts == PARTS and dates == 2 * GROUP
        groups = dates // GROUP
        pieces = 1 + dates + groups
        held = 4 * lines * cols * (LAG_MAX * dates + 3 * dates + 1) + 4 * 8 * LANES
        height = lines + ROWS
        inside = pl.BlockSpec(memory_space=pltpu.VMEM)
        anywhere = pl.BlockSpec(memory_space=pltpu.HBM)
        field = (lines, cols)
        dma = pltpu.SemaphoreType.DMA
        coh, logs, mean, total, lags = pl.pallas_call(
            functools.partial(gather_kernel, (dates_axis, rng_axis, dates, lines, cols)),
            out_shape=[
                jax.ShapeDtypeStruct((2 * dates, LAG_MAX, *field), BF16),
                jax.ShapeDtypeStruct((2 * dates, *field), F32),
                jax.ShapeDtypeStruct((dates, *field), F32),
                jax.ShapeDtypeStruct(field, F32),
                jax.ShapeDtypeStruct(lags.shape, lags.dtype),
            ],
            in_specs=[anywhere] * 2,
            out_specs=[inside] * 5,
            scratch_shapes=[
                pltpu.VMEM((2 * dates, parts, BLOCKS, height, LANES), BF16),
                pltpu.VMEM((groups, sides, height, LANES), BF16),
                pltpu.VMEM((2, groups, sides, height, LANES), BF16),
                pltpu.VMEM((2, sides, parts, height, LANES), BF16),
                pltpu.VMEM((2, sides, lines, LANES), F32),
                pltpu.VMEM((2, sides, LAG_MAX, parts, lines, LANES), F32),
                pltpu.VMEM((cols, cols), BF16),
                pltpu.VMEM((sides, LANES, LANES), BF16),
                pltpu.VMEM((lines, height), BF16),
                pltpu.VMEM((2 * dates, *field), F32),
                pltpu.VMEM(field, F32),
                pltpu.VMEM((2, *field), BF16),
                pltpu.VMEM((2, *field), BF16),
                dma((BLOCKS,)), dma, dma((pieces, BLOCKS)), dma((pieces, BLOCKS)),
                dma((1 + groups, BLOCKS)), dma((1 + groups, BLOCKS)),
                dma((sides, groups, 2)), dma((sides, groups, 2)),
                dma((2,)), dma((2,)),
            ],
            compiler_params=pltpu.CompilerParams(collective_id=0, has_side_effects=True, vmem_limit_bytes=VMEM_BYTES - SPARE - held),
            name="gather",
        )(pltpu.with_memory_space_constraint(slc, pltpu.HBM), pltpu.with_memory_space_constraint(lags, pltpu.HBM))
        return pl.pallas_call(
            functools.partial(pick_kernel, (dates, slots, lines, cols)),
            out_shape=[
                jax.ShapeDtypeStruct((dates, slots, *field), BF16),
                jax.ShapeDtypeStruct((dates, slots, *field), BF16),
                jax.ShapeDtypeStruct((dates, *field), F32),
            ],
            in_specs=[inside] * 5,
            out_specs=[anywhere] * 3,
            scratch_shapes=[
                pltpu.SMEM((dates, slots), jnp.int32),
                pltpu.VMEM((dates, slots, *field), BF16),
                pltpu.VMEM((dates, *field), F32),
                dma, dma, dma, dma,
            ],
            compiler_params=pltpu.CompilerParams(vmem_limit_bytes=16 * 2 ** 20),
            name="pick",
        )(lags, coh, logs, mean, total)

    return jax.shard_map(
        on_device,
        mesh=mesh,
        in_specs=(P(("slab", "date"), None, "az", "rng"), P("date", None)),
        out_specs=(
            P(("slab", "date"), None, "az", "rng"),
            P(("slab", "date"), None, "az", "rng"),
            P(("slab", "date"), "az", "rng"),
        ),
        check_vma=False,
    )
```
